256 devices in a mesh: dp: 16 (over z, core), expert: 16 (over y, x).
Axes of the slice: x: 4, y: 4, z: 8, core: 2. Of those that a mesh axis runs over, the one named last changes fastest.
Arguments:
- tokens: bfloat16 [16384, 2048], P(('dp', 'expert')), parts along dimension 0, may hold values from -6 to 6
- router_weight: bfloat16 [2048, 16], replicated, may hold values from -0.125 to 0.125
- gate_weight: bfloat16 [16, 2048, 768], P('expert'), may hold values from -0.125 to 0.125
- up_weight: bfloat16 [16, 2048, 768], P('expert'), may hold values from -0.125 to 0.125
- down_weight: bfloat16 [16, 768, 2048], P('expert'), may hold values from -0.21875 to 0.21875
- routing: int32 [16384, 4], P(('dp', 'expert')), parts along dimension 0, may hold values from 0 to 15, as said below
- priority: int32 [256, 256], P(('dp', 'expert')), parts along dimension 0, may hold values from 0 to 255, each once within a row
- hot_list: int32 [32], P('dp'), parts along dimension 0, may hold values from 0 to 15, as said below
Outputs:
- mixed: bfloat16 [16384, 2048], P(('dp', 'expert')), parts along dimension 0
The draws below stay inside these ranges and needn't reach their ends.
There are 16 independent parts, one for each index of `dp`. The reference program is written for one: setup_inputs(seed, part) draws one part's arguments, and reference() takes and returns one part's arrays. A program takes and returns all parts, laid end to end along the dimension named above; an argument that names none is the same for every part. Nothing has to cross between parts.
Inputs may be any that keep to these rules, and one draw needn't show every extreme that they name: `routing`: each token names 4 different experts. `priority`: each row is a permutation. `hot_list`: 2 different experts.
All inputs are finite; a program needn't handle non-finite values.
Results may differ from the reference program's by a relative error of at most 0.0085.
Values may be sent and summed in bfloat16 or wider, within the bound.
A program may use at most 64 MiB of HBM per device.

```python
import jax
import jax.numpy as jnp
from jax import lax

D = 2048
FF = 768
TOK_DEV = 64
TOPK = 4
HOT = 2
EXPERTS = 16
TOKENS = 1024
SLOTS = 256
CAP = 24
N_EXPERT = 16


def routing_and_hot(key):
    base = jax.random.fold_in(key, 11)
    order = jax.random.permutation(jax.random.fold_in(base, 1), EXPERTS).astype(jnp.int32)
    place = jnp.argsort(order).astype(jnp.int32)
    pull = jnp.where(place < HOT, 3000, jnp.where(place < 2 * HOT, 2400, 1200 * (EXPERTS - place) // EXPERTS)).astype(jnp.int32)
    tickets = jax.random.randint(jax.random.fold_in(base, 2), (TOKENS, EXPERTS), 0, 4096, dtype=jnp.int32)
    labels = jnp.arange(EXPERTS, dtype=jnp.int32)
    scores = (tickets + pull[None, :]) * EXPERTS + labels[None, :]
    values, chosen = lax.top_k(scores, TOPK)
    return (chosen.astype(jnp.int32), order[:HOT])


def draw_routing(key, part):
    return routing_and_hot(key)[0]


def draw_hot_list(key, part):
    return routing_and_hot(key)[1]


def levels(stream_key, shape, pieces, smallest, high):
    gain = 1.0
    for axis_at, blocks in pieces:
        heights = jax.random.uniform(jax.random.fold_in(jax.random.fold_in(stream_key, 6), axis_at), (blocks,), jnp.float32, smallest / len(pieces), high / len(pieces))
        gain = gain * jnp.repeat(jnp.exp(heights), shape[axis_at] // blocks).reshape((-1,) + (1,) * (len(shape) - 1 - axis_at))
    return gain


def centred(stream_key, extent, spread, limit, shards=(), held_as=jnp.bfloat16):
    entries = jax.random.normal(stream_key, extent, jnp.float32) * spread
    if len(shards) > 0:
        entries = levels(stream_key, extent, shards, -0.22, 0.18) * entries
    return jnp.clip(entries, min=-limit, max=limit).astype(held_as)


def setup_inputs(seed: int = 0, part: int = 0) -> dict:
    splits = jax.random.split(jax.random.key(seed), 9)
    own_keys = jax.random.split(jax.random.fold_in(splits[8], part), 9)
    tokens = centred(own_keys[0], (TOKENS, D), 1.0, 6.0, ((0, 16),))
    router_weight = centred(splits[1], (D, EXPERTS), D ** -0.5, 0.125)
    gate_weight = centred(splits[2], (EXPERTS, D, FF), D ** -0.5, 0.125, ((0, 16),))
    up_weight = centred(splits[3], (EXPERTS, D, FF), D ** -0.5, 0.125, ((0, 16),))
    down_weight = centred(splits[4], (EXPERTS, FF, D), FF ** -0.5, 0.21875, ((0, 16),))
    routing = draw_routing(jax.random.fold_in(jax.random.fold_in(splits[8], part), 71), part)
    priority = jax.vmap(lambda own: jax.random.permutation(own, SLOTS))(jax.random.split(own_keys[6], N_EXPERT)).reshape((N_EXPERT, SLOTS)).astype(jnp.int32)
    hot_list = draw_hot_list(jax.random.fold_in(jax.random.fold_in(splits[8], part), 71), part)
    return dict(tokens=tokens, router_weight=router_weight, gate_weight=gate_weight, up_weight=up_weight, down_weight=down_weight, routing=routing, priority=priority, hot_list=hot_list)


def expert_swiglu(inputs, gate_mat, up_mat, down_mat):
    gate_part = jnp.dot(inputs, gate_mat, preferred_element_type=jnp.float32)
    up_part = jnp.dot(inputs, up_mat, preferred_element_type=jnp.float32)
    hidden = (jax.nn.silu(gate_part) * up_part).astype(jnp.bfloat16)
    return jnp.dot(hidden, down_mat, preferred_element_type=jnp.float32).astype(jnp.bfloat16)


def reference(tokens, router_weight, gate_weight, up_weight, down_weight, routing, priority, hot_list):
    logits = jnp.dot(tokens, router_weight, preferred_element_type=jnp.float32)
    chosen = jnp.take_along_axis(logits, routing, axis=1)
    sigmas = jax.nn.sigmoid(chosen)
    weights = sigmas / jnp.sum(sigmas, axis=1, keepdims=True)
    hot_flag = jnp.any(routing[:, :, None] == hot_list[None, None, :], axis=2)
    block_expert = routing.reshape(N_EXPERT, TOK_DEV * TOPK)
    block_hot = hot_flag.reshape(N_EXPERT, TOK_DEV * TOPK)
    same_expert = block_expert[:, :, None] == block_expert[:, None, :]
    earlier = priority[:, None, :] < priority[:, :, None]
    ranks = jnp.sum((same_expert & earlier).astype(jnp.int32), axis=2)
    keeping = block_hot | (ranks < CAP)
    kept = jnp.where(keeping.reshape(TOKENS, TOPK), weights, jnp.float32(0.0))

    def add_expert(index, total):
        answer = expert_swiglu(tokens, gate_weight[index], up_weight[index], down_weight[index])
        share = jnp.sum(jnp.where(routing == index, kept, jnp.float32(0.0)), axis=1)
        return total + share[:, None] * answer.astype(jnp.float32)

    total = lax.fori_loop(0, EXPERTS, add_expert, jnp.zeros((TOKENS, D), jnp.float32))
    return total.astype(jnp.bfloat16)
```

```python
import functools

import jax
import jax.numpy as jnp
from jax import lax
from jax.experimental import pallas as pl
from jax.experimental.pallas import tpu as pltpu
from jax.sharding import PartitionSpec as P

MESH = pl.DeviceIdType.MESH
SIDE = 4
LO, HI = pl.ds(0, 16), pl.ds(16, 16)
N_SEMS = 128
FAR = 4096.0


def kernel(
    tokens, router, gate, up, down, routing, priority, hot_list, out,
    grid_tok, part, relay, final, summed, relay2, final2, shares, columns,
    w_gate, w_up, w_down, w_router, own, hidden, result, route_v, prio_v, hot_s,
    send_sem, recv_sem, local_sem,
):
    me = lax.axis_index("expert")
    my_y, my_x = me // SIDE, me % SIDE
    x_plus = my_y * SIDE + (my_x + 1) % SIDE
    x_minus = my_y * SIDE + (my_x + SIDE - 1) % SIDE
    y_plus = ((my_y + 1) % SIDE) * SIDE + my_x
    y_minus = ((my_y + SIDE - 1) % SIDE) * SIDE + my_x
    first = ((x_plus, x_minus), (y_plus, y_minus))
    second = ((y_plus, y_minus), (x_plus, x_minus))
    half = own.shape[1]
    n_ff = w_gate.shape[1]
    width = w_gate.shape[0]
    n_exp = SIDE * SIDE
    capacity = min(2 * half, 3 * prio_v.shape[1] // (2 * n_exp))

    copies = []

    def remote(src, dst, device):
        index = len(copies)
        made = pltpu.make_async_remote_copy(
            src_ref=src, dst_ref=dst, send_sem=send_sem.at[index], recv_sem=recv_sem.at[index],
            device_id={"expert": device}, device_id_type=MESH,
        )
        copies.append(made)
        made.start()
        return made

    local_count = [0]

    def local(src, dst):
        made = pltpu.make_async_copy(src, dst, local_sem.at[local_count[0]])
        local_count[0] += 1
        made.start()
        return made

    barrier = pltpu.get_barrier_semaphore()
    for device in (x_plus, x_minus, y_plus, y_minus):
        pl.semaphore_signal(barrier, inc=1, device_id={"expert": device}, device_id_type=MESH)
    own_in = [local(tokens.at[pl.ds(s * half, half)], own.at[s]) for s in range(2)]
    route_in = local(routing, route_v)
    prio_in = local(priority, prio_v)
    hot_in = local(hot_list, hot_s)
    router_in = local(router, w_router)
    slot_in = [
        local(tokens.at[pl.ds(s * half, half)], grid_tok.at[0, s, 0]) for s in range(2)
    ]
    pl.semaphore_wait(barrier, 4)

    ag1 = [None, None]
    ag2 = [[None] * SIDE, [None] * SIDE]
    ag2f = [[None] * SIDE, [None] * SIDE]
    for s in range(2):
        mine = tokens.at[pl.ds(s * half, half)]
        ag1[s] = (
            remote(mine, grid_tok.at[3, s, 0], first[s][0]),
            remote(mine, grid_tok.at[1, s, 0], first[s][1]),
        )
    for s in range(2):
        mine = tokens.at[pl.ds(s * half, half)]
        ag2[s][0] = (
            remote(mine, grid_tok.at[0, s, 3], second[s][0]),
            remote(mine, grid_tok.at[0, s, 1], second[s][1]),
        )
    gate_in = local(gate.at[0], w_gate)
    up_in = local(up.at[0], w_up)
    down_in = local(down.at[0], w_down)

    for made in own_in:
        made.wait()
    route_in.wait()
    prio_in.wait()
    hot_in.wait()
    router_in.wait()
    toks = 2 * half
    logits = jnp.concatenate(
        [jnp.dot(own[s], w_router[...], preferred_element_type=jnp.float32) for s in range(2)], axis=0
    )
    logits = jnp.concatenate(
        [logits, jnp.zeros((toks, 128 - n_exp), jnp.float32)], axis=1
    )
    sigmas = jax.nn.sigmoid(logits)
    lanes = lax.broadcasted_iota(jnp.int32, (toks, 128), 1)
    slot_at = lax.broadcasted_iota(jnp.int32, (toks, prio_v.shape[1]), 1)
    slot_of = lax.broadcasted_iota(jnp.int32, (toks, prio_v.shape[1]), 0) * SIDE
    order = jnp.broadcast_to(prio_v[...].astype(jnp.float32), (toks, prio_v.shape[1]))
    prior = jnp.full((toks, 128), FAR, jnp.float32)
    picked = jnp.zeros((toks, 128), jnp.float32)
    for k in range(route_v.shape[1]):
        hit = route_v[:, k : k + 1] == lanes
        place = jnp.sum(jnp.where(slot_at == slot_of + k, order, 0.0), axis=1, keepdims=True)
        prior = jnp.where(hit, place, prior)
        picked = jnp.where(hit, sigmas, picked)
    weights = picked / jnp.sum(picked, axis=1, keepdims=True)
    fill = jnp.full((128 - toks, 128), FAR, jnp.float32)
    prior_t = jnp.transpose(jnp.concatenate([prior, fill], axis=0))[:n_exp]
    weight_t = jnp.transpose(jnp.concatenate([weights, fill], axis=0))[:n_exp]
    experts = lax.broadcasted_iota(jnp.int32, (n_exp, 128), 0)
    rank_rows = []
    for e in range(n_exp):
        before = prior[:, e : e + 1] < prior_t[e : e + 1, :]
        rank_rows.append(jnp.sum(jnp.where(before, 1.0, 0.0), axis=0, keepdims=True))
    ranks = jnp.concatenate(rank_rows, axis=0)
    hot = (experts == hot_s[0]) | (experts == hot_s[1])
    token_at = lax.broadcasted_iota(jnp.int32, (n_exp, 128), 1)
    keep = (hot | (ranks < capacity)) & (token_at < toks)
    kept = jnp.where(keep, weight_t, 0.0)
    shares[0, 0] = kept[:8] + pltpu.roll(kept[8:], 64, axis=1)

    def forward_first(s):
        ag1[s][0].wait_recv()
        plus = remote(grid_tok.at[3, s, 0, LO], grid_tok.at[2, s, 0, LO], first[s][0])
        ag1[s][1].wait_recv()
        minus = remote(grid_tok.at[1, s, 0, HI], grid_tok.at[2, s, 0, HI], first[s][1])
        return plus, minus

    def spread(s, d):
        ag2[s][d] = (
            remote(grid_tok.at[d, s, 0], grid_tok.at[d, s, 3], second[s][0]),
            remote(grid_tok.at[d, s, 0], grid_tok.at[d, s, 1], second[s][1]),
        )

    def forward_second(s, d):
        ag2[s][d][0].wait_recv()
        plus = remote(grid_tok.at[d, s, 3, LO], grid_tok.at[d, s, 2, LO], second[s][0])
        ag2[s][d][1].wait_recv()
        minus = remote(grid_tok.at[d, s, 1, HI], grid_tok.at[d, s, 2, HI], second[s][1])
        ag2f[s][d] = (plus, minus)

    share_x = (
        remote(shares.at[0, 0], shares.at[3, 0], x_plus),
        remote(shares.at[0, 0], shares.at[1, 0], x_minus),
    )
    ag1f = [forward_first(s) for s in range(2)]
    for s in range(2):
        spread(s, 3)
    for s in range(2):
        spread(s, 1)
    share_x[0].wait_recv()
    share_x2 = remote(shares.at[3, 0], shares.at[2, 0], x_plus)
    for s in range(2):
        forward_second(s, 0)
    for s in range(2):
        ag1f[s][0].wait_recv()
        ag1f[s][1].wait_recv()
        spread(s, 2)
    share_x[1].wait_recv()
    share_x2.wait_recv()
    share_y = (
        remote(shares.at[:, 0], shares.at[:, 3], y_plus),
        remote(shares.at[:, 0], shares.at[:, 1], y_minus),
    )
    for s in range(2):
        forward_second(s, 3)
    share_y[0].wait_recv()
    share_y2 = remote(shares.at[:, 3], shares.at[:, 2], y_plus)
    for s in range(2):
        slot_in[s].wait()
    gate_in.wait()
    up_in.wait()
    down_in.wait()
    share_y[1].wait_recv()
    share_y2.wait_recv()

    my_row, my_half = me % 8, me // 8
    share_row = lax.broadcasted_iota(jnp.int32, (8, 128), 0) == my_row
    token_lane = lax.broadcasted_iota(jnp.int32, (half, 128), 1)
    token_row = lax.broadcasted_iota(jnp.int32, (half, 128), 0)

    def expert(d):
        for s in range(2):
            pick = token_lane == token_row + (my_half * 64 + s * half)
            for e in range(SIDE):
                held = shares[d, e] if s == 0 else shares[e, d]
                row = jnp.sum(jnp.where(share_row, held, 0.0), axis=0, keepdims=True)
                row = jnp.broadcast_to(row, (half, 128))
                columns[pl.ds((s * SIDE + e) * half, half)] = jnp.broadcast_to(
                    jnp.sum(jnp.where(pick, row, 0.0), axis=1, keepdims=True), (half, 128)
                )
        rows = 2 * SIDE * half

        def inner(n, carry):
            at = pl.ds(pl.multiple_of(n * 256, 256), 256)
            block = grid_tok[d].reshape(rows, width)
            g = jnp.dot(block, w_gate[:, at], preferred_element_type=jnp.float32)
            u = jnp.dot(block, w_up[:, at], preferred_element_type=jnp.float32)
            hidden[:, at] = (g / (1.0 + jnp.exp(-g)) * u).astype(jnp.bfloat16)
            return carry

        lax.fori_loop(0, n_ff // 256, inner, 0)

        def outer(n, carry):
            at = pl.ds(pl.multiple_of(n * 256, 256), 256)
            o = jnp.dot(hidden[...], w_down[:, at], preferred_element_type=jnp.float32)
            scale = jnp.concatenate([columns[...], columns[...]], axis=1)
            part[d, :, :, :, at] = (o * scale).astype(jnp.bfloat16).reshape(2, SIDE, half, 256)
            return carry

        lax.fori_loop(0, width // 256, outer, 0)

    rs1f = [[None] * SIDE, [None] * SIDE]
    rs1 = [[None] * SIDE, [None] * SIDE]

    def reduce_start(s, d):
        rs1f[s][d] = (
            remote(part.at[d, s, 2, LO], relay.at[d, s, 0], second[s][0]),
            remote(part.at[d, s, 2, HI], relay.at[d, s, 1], second[s][1]),
        )
        rs1[s][d] = [
            remote(part.at[d, s, 1, HI], final.at[d, s, 0, HI], second[s][0]),
            remote(part.at[d, s, 3, LO], final.at[d, s, 1, LO], second[s][1]),
        ]

    def total(*values):
        result = values[0].astype(jnp.float32)
        for value in values[1:]:
            result = result + value.astype(jnp.float32)
        return result

    def reduce_relay(s, d):
        rs1f[s][d][0].wait_recv()
        part[d, s, 1, LO] = total(part[d, s, 1, LO], relay[d, s, 0]).astype(jnp.bfloat16)
        rs1f[s][d][1].wait_recv()
        part[d, s, 3, HI] = total(part[d, s, 3, HI], relay[d, s, 1]).astype(jnp.bfloat16)
        rs1[s][d] += [
            remote(part.at[d, s, 1, LO], final.at[d, s, 0, LO], second[s][0]),
            remote(part.at[d, s, 3, HI], final.at[d, s, 1, HI], second[s][1]),
        ]

    def reduce_finish(s, d):
        for made in rs1[s][d]:
            made.wait_recv()
        summed[d, s] = total(part[d, s, 0], final[d, s, 0], final[d, s, 1]).astype(jnp.bfloat16)

    for s in range(2):
        ag2f[s][0][0].wait_recv()
        ag2f[s][0][1].wait_recv()
    expert(0)
    for s in range(2):
        reduce_start(s, 0)
    for s in range(2):
        forward_second(s, 1)
    for s in range(2):
        forward_second(s, 2)
    for s in range(2):
        ag2f[s][3][0].wait_recv()
        ag2f[s][3][1].wait_recv()
    expert(3)
    for s in range(2):
        reduce_start(s, 3)
    for s in range(2):
        reduce_relay(s, 0)
    for s in range(2):
        ag2f[s][1][0].wait_recv()
        ag2f[s][1][1].wait_recv()
    expert(1)
    for s in range(2):
        reduce_start(s, 1)
    for s in range(2):
        reduce_relay(s, 3)
    for s in range(2):
        ag2f[s][2][0].wait_recv()
        ag2f[s][2][1].wait_recv()
    expert(2)
    for s in range(2):
        reduce_start(s, 2)
    for s in range(2):
        reduce_relay(s, 1)
    for s in range(2):
        reduce_relay(s, 2)
    rs2 = [None, None]
    rs2f = [None, None]
    for d in (0, 3, 1):
        for s in range(2):
            reduce_finish(s, d)
    for s in range(2):
        rs2[s] = [
            remote(summed.at[1, s, HI], final2.at[s, 0, HI], first[s][0]),
            remote(summed.at[3, s, LO], final2.at[s, 1, LO], first[s][1]),
        ]
    for s in range(2):
        reduce_finish(s, 2)
    for s in range(2):
        rs2f[s] = (
            remote(summed.at[2, s, LO], relay2.at[s, 0], first[s][0]),
            remote(summed.at[2, s, HI], relay2.at[s, 1], first[s][1]),
        )
    for s in range(2):
        rs2f[s][0].wait_recv()
        summed[1, s, LO] = total(summed[1, s, LO], relay2[s, 0]).astype(jnp.bfloat16)
        rs2f[s][1].wait_recv()
        summed[3, s, HI] = total(summed[3, s, HI], relay2[s, 1]).astype(jnp.bfloat16)
        rs2[s] += [
            remote(summed.at[1, s, LO], final2.at[s, 0, LO], first[s][0]),
            remote(summed.at[3, s, HI], final2.at[s, 1, HI], first[s][1]),
        ]
    for s in range(2):
        for made in rs2[s]:
            made.wait_recv()
        result[pl.ds(s * half, half)] = total(
            summed[0, s], final2[s, 0], final2[s, 1]
        ).astype(jnp.bfloat16)
    out_copy = local(result, out)
    for made in copies:
        made.wait_send()
    out_copy.wait()


def shards(tokens, router_weight, gate_weight, up_weight, down_weight, routing, priority, hot_list):
    toks, width = tokens.shape
    half = toks // 2
    n_ff = gate_weight.shape[2]
    bf16, f32 = jnp.bfloat16, jnp.float32
    any_spec = pl.BlockSpec(memory_space=pl.ANY)
    return pl.pallas_call(
        kernel,
        out_shape=jax.ShapeDtypeStruct((toks, width), bf16),
        in_specs=[any_spec] * 8,
        out_specs=any_spec,
        scratch_shapes=[
            pltpu.VMEM((SIDE, 2, SIDE, half, width), bf16),
            pltpu.VMEM((SIDE, 2, SIDE, half, width), bf16),
            pltpu.VMEM((SIDE, 2, 2, half // 2, width), bf16),
            pltpu.VMEM((SIDE, 2, 2, half, width), bf16),
            pltpu.VMEM((SIDE, 2, half, width), bf16),
            pltpu.VMEM((2, 2, half // 2, width), bf16),
            pltpu.VMEM((2, 2, half, width), bf16),
            pltpu.VMEM((SIDE, SIDE, 8, 128), f32),
            pltpu.VMEM((2 * SIDE * half, 128), f32),
            pltpu.VMEM((width, n_ff), bf16),
            pltpu.VMEM((width, n_ff), bf16),
            pltpu.VMEM((n_ff, width), bf16),
            pltpu.VMEM(router_weight.shape, bf16),
            pltpu.VMEM((2, half, width), bf16),
            pltpu.VMEM((2 * SIDE * half, n_ff), bf16),
            pltpu.VMEM((toks, width), bf16),
            pltpu.VMEM(routing.shape, jnp.int32),
            pltpu.VMEM(priority.shape, jnp.int32),
            pltpu.SMEM(hot_list.shape, jnp.int32),
            pltpu.SemaphoreType.DMA((N_SEMS,)),
            pltpu.SemaphoreType.DMA((N_SEMS,)),
            pltpu.SemaphoreType.DMA((16,)),
        ],
        compiler_params=pltpu.CompilerParams(
            collective_id=0, has_side_effects=True, vmem_limit_bytes=48 * 1024 * 1024
        ),
    )(tokens, router_weight, gate_weight, up_weight, down_weight, routing, priority, hot_list)


def solution(mesh):
    return jax.shard_map(
        shards,
        mesh=mesh,
        in_specs=(
            P(("dp", "expert"), None),
            P(),
            P("expert", None, None),
            P("expert", None, None),
            P("expert", None, None),
            P(("dp", "expert"), None),
            P(("dp", "expert"), None),
            P("dp"),
        ),
        out_specs=P(("dp", "expert"), None),
        check_vma=False,
    )
```

```python
import jax
import jax.numpy as jnp
from jax import lax
from jax.experimental import pallas as pl
from jax.experimental.pallas import tpu as pltpu
from jax.sharding import PartitionSpec as P

MESH = pl.DeviceIdType.MESH
SIDE = 4
LO, HI = pl.ds(0, 16), pl.ds(16, 16)
N_SEMS = 128
FAR = 4096.0
ORDER = (
    ("O", 1), ("O", 0), ("S", 0, 0), ("S", 0, 1), ("X",), ("f", 0, 1), ("f", 0, 0), ("f", 1, 0),
    ("f", 1, 1), ("S", 3, 0), ("S", 3, 1), ("g", 1, 0, 0), ("g", 0, 0, 0), ("g", 0, 0, 1),
    ("g", 1, 0, 1), ("Y",), ("S", 2, 1), ("S", 2, 0), ("g", 0, 3, 1), ("g", 1, 3, 1), ("g", 0, 3, 0),
    ("g", 1, 3, 0), ("S", 1, 1), ("S", 1, 0), ("E", 0, 0), ("E", 0, 1), ("g", 1, 2, 1), ("g", 1, 2, 0),
    ("g", 0, 2, 1), ("g", 0, 2, 0), ("E", 3, 1), ("b", 0, 1), ("b", 0, 0), ("E", 3, 0), ("b", 3, 1),
    ("a", 3, 0), ("g", 0, 1, 1), ("g", 1, 1, 1), ("g", 0, 1, 0), ("g", 1, 1, 0), ("E", 2, 1),
    ("b", 2, 1), ("E", 2, 0), ("b", 2, 0), ("a", 2, 0), ("a", 2, 1), ("r", 0, 3, 0), ("a", 3, 1),
    ("r", 1, 3, 0), ("E", 1, 1), ("a", 1, 1), ("E", 1, 0), ("a", 1, 0), ("b", 3, 0), ("r", 0, 2, 1),
    ("r", 1, 2, 1), ("b", 1, 1), ("r", 0, 2, 0), ("r", 1, 2, 0), ("r", 0, 3, 1), ("r", 1, 3, 1),
    ("b", 1, 0), ("r", 0, 1, 1), ("r", 1, 1, 1), ("r", 0, 1, 0), ("r", 1, 1, 0), ("F", 2, 1), ("A", 1),
    ("F", 3, 0), ("a", 0, 1), ("F", 2, 0), ("A", 0), ("a", 0, 0), ("F", 3, 1), ("B", 0, 0), ("B", 0, 1),
    ("F", 1, 1), ("B", 1, 1), ("F", 1, 0), ("B", 1, 0), ("r", 0, 0, 1), ("r", 1, 0, 1), ("R", 0, 1),
    ("R", 1, 1), ("R", 0, 0), ("R", 1, 0), ("r", 0, 0, 0), ("r", 1, 0, 0), ("Z", 1), ("Z", 0),
)


def kernel(
    tokens, router, gate, up, down, routing, priority, hot_list, out,
    grid_tok, part, relay, final, summed, relay2, final2, shares, columns,
    w_gate, w_up, w_down, w_router, own, hidden, result, route_v, prio_v, hot_s,
    send_sem, recv_sem, local_sem, far_sem,
):
    me = lax.axis_index("expert")
    my_y, my_x = me // SIDE, me % SIDE
    x_plus = my_y * SIDE + (my_x + 1) % SIDE
    x_minus = my_y * SIDE + (my_x + SIDE - 1) % SIDE
    y_plus = ((my_y + 1) % SIDE) * SIDE + my_x
    y_minus = ((my_y + SIDE - 1) % SIDE) * SIDE + my_x
    x_far = my_y * SIDE + (my_x + 2) % SIDE
    y_far = ((my_y + 2) % SIDE) * SIDE + my_x
    first = ((x_plus, x_minus), (y_plus, y_minus))
    second = ((y_plus, y_minus), (x_plus, x_minus))
    half = own.shape[1]
    n_ff = w_gate.shape[1]
    width = w_gate.shape[0]
    n_exp = SIDE * SIDE
    capacity = min(2 * half, 3 * prio_v.shape[1] // (2 * n_exp))

    copies, landed = {}, set()

    def remote(key, src, dst, device):
        index = len(copies)
        copies[key] = pltpu.make_async_remote_copy(
            src_ref=src, dst_ref=dst, send_sem=send_sem.at[index], recv_sem=recv_sem.at[index],
            device_id={"expert": device}, device_id_type=MESH,
        )
        copies[key].start()

    def got(*keys):
        for key in keys:
            if key not in landed:
                landed.add(key)
                copies[key].wait_recv()

    local_count = [0]

    def local(src, dst):
        made = pltpu.make_async_copy(src, dst, local_sem.at[local_count[0]])
        local_count[0] += 1
        made.start()
        return made

    barrier = pltpu.get_barrier_semaphore()
    for device in (x_plus, x_minus, y_plus, y_minus):
        pl.semaphore_signal(barrier, inc=1, device_id={"expert": device}, device_id_type=MESH)
    own_in = [local(tokens.at[pl.ds(s * half, half)], own.at[s]) for s in range(2)]
    small_in = [
        local(routing, route_v), local(priority, prio_v), local(hot_list, hot_s), local(router, w_router)
    ]
    pl.semaphore_wait(barrier, 4)

    def own_first(s):
        mine = tokens.at[pl.ds(s * half, half)]
        remote(("O+", s), mine, grid_tok.at[3, s, 0], first[s][0])
        remote(("O-", s), mine, grid_tok.at[1, s, 0], first[s][1])

    def spread(d, s):
        if d == 0:
            mine = tokens.at[pl.ds(s * half, half)]
        else:
            got(*{3: [("O+", s)], 1: [("O-", s)], 2: [("f+", s), ("f-", s)]}[d])
            mine = grid_tok.at[d, s, 0]
        remote(("S+", d, s), mine, grid_tok.at[d, s, 3], second[s][0])
        remote(("S-", d, s), mine, grid_tok.at[d, s, 1], second[s][1])

    def pass_first(plus, s):
        if plus:
            got(("O+", s))
            remote(("f+", s), grid_tok.at[3, s, 0, LO], grid_tok.at[2, s, 0, LO], first[s][0])
        else:
            got(("O-", s))
            remote(("f-", s), grid_tok.at[1, s, 0, HI], grid_tok.at[2, s, 0, HI], first[s][1])

    def pass_second(plus, d, s):
        if plus:
            got(("S+", d, s))
            remote(("g+", d, s), grid_tok.at[d, s, 3, LO], grid_tok.at[d, s, 2, LO], second[s][0])
        else:
            got(("S-", d, s))
            remote(("g-", d, s), grid_tok.at[d, s, 1, HI], grid_tok.at[d, s, 2, HI], second[s][1])

    def share_x():
        make_shares()
        pl.semaphore_wait(far_sem.at[0], 1)
        remote("X+", shares.at[0, 0], shares.at[3, 0], x_plus)
        remote("X-", shares.at[0, 0], shares.at[1, 0], x_minus)
        remote("X2", shares.at[0, 0], shares.at[2, 0], x_far)

    def share_y():
        got("X+", "X-", "X2")
        pl.semaphore_wait(far_sem.at[1], 1)
        remote("Y+", shares.at[:, 0], shares.at[:, 3], y_plus)
        remote("Y-", shares.at[:, 0], shares.at[:, 1], y_minus)
        remote("Y2", shares.at[:, 0], shares.at[:, 2], y_far)

    my_row, my_half = me % 8, me // 8
    rows = SIDE * half
    loaded = []

    def expert(d, s):
        if not loaded:
            got("X+", "X-", "X2", "Y+", "Y-", "Y2")
            for made in heavy_in:
                made.wait()
            loaded.append(1)
        got(("S+", d, s), ("S-", d, s), ("g+", d, s), ("g-", d, s))
        got(*{0: [], 3: [("O+", s)], 1: [("O-", s)], 2: [("f+", s), ("f-", s)]}[d])
        share_row = lax.broadcasted_iota(jnp.int32, (8, 128), 0) == my_row
        token_lane = lax.broadcasted_iota(jnp.int32, (half, 128), 1)
        token_row = lax.broadcasted_iota(jnp.int32, (half, 128), 0)
        pick = token_lane == token_row + (my_half * 64 + s * half)
        for e in range(SIDE):
            held = shares[d, e] if s == 0 else shares[e, d]
            row = jnp.sum(jnp.where(share_row, held, 0.0), axis=0, keepdims=True)
            row = jnp.broadcast_to(row, (half, 128))
            columns[pl.ds(e * half, half)] = jnp.broadcast_to(
                jnp.sum(jnp.where(pick, row, 0.0), axis=1, keepdims=True), (half, 128)
            )
        for n in range(n_ff // 256):
            at = pl.ds(n * 256, 256)
            block = grid_tok[d, s].reshape(rows, width)
            g = jnp.dot(block, w_gate[:, at], preferred_element_type=jnp.float32)
            u = jnp.dot(block, w_up[:, at], preferred_element_type=jnp.float32)
            hidden[:, at] = (g / (1.0 + jnp.exp(-g)) * u).astype(jnp.bfloat16)
        for n in range(width // 256):
            at = pl.ds(n * 256, 256)
            o = jnp.dot(hidden[...], w_down[:, at], preferred_element_type=jnp.float32)
            scale = jnp.concatenate([columns[...], columns[...]], axis=1)
            part[d, s, :, :, at] = (o * scale).astype(jnp.bfloat16).reshape(SIDE, half, 256)

    def total(*values):
        result = values[0].astype(jnp.float32)
        for value in values[1:]:
            result = result + value.astype(jnp.float32)
        return result

    def far_halves(d, s):
        remote(("a+", d, s), part.at[d, s, 2, LO], relay.at[d, s, 0], second[s][0])
        remote(("a-", d, s), part.at[d, s, 2, HI], relay.at[d, s, 1], second[s][1])

    def near_halves(d, s):
        remote(("b+", d, s), part.at[d, s, 1, HI], final.at[d, s, 0, HI], second[s][0])
        remote(("b-", d, s), part.at[d, s, 3, LO], final.at[d, s, 1, LO], second[s][1])

    def add_second(plus, d, s):
        if plus:
            got(("a+", d, s))
            part[d, s, 1, LO] = total(part[d, s, 1, LO], relay[d, s, 0]).astype(jnp.bfloat16)
            remote(("r+", d, s), part.at[d, s, 1, LO], final.at[d, s, 0, LO], second[s][0])
        else:
            got(("a-", d, s))
            part[d, s, 3, HI] = total(part[d, s, 3, HI], relay[d, s, 1]).astype(jnp.bfloat16)
            remote(("r-", d, s), part.at[d, s, 3, HI], final.at[d, s, 1, HI], second[s][1])

    def fold(d, s):
        got(("b+", d, s), ("b-", d, s), ("r+", d, s), ("r-", d, s))
        summed[d, s] = total(part[d, s, 0], final[d, s, 0], final[d, s, 1]).astype(jnp.bfloat16)

    def far_first(s):
        remote(("A+", s), summed.at[2, s, LO], relay2.at[s, 0], first[s][0])
        remote(("A-", s), summed.at[2, s, HI], relay2.at[s, 1], first[s][1])

    def near_first(plus, s):
        if plus:
            remote(("B+", s), summed.at[1, s, HI], final2.at[s, 0, HI], first[s][0])
        else:
            remote(("B-", s), summed.at[3, s, LO], final2.at[s, 1, LO], first[s][1])

    def add_first(plus, s):
        if plus:
            got(("A+", s))
            summed[1, s, LO] = total(summed[1, s, LO], relay2[s, 0]).astype(jnp.bfloat16)
            remote(("R+", s), summed.at[1, s, LO], final2.at[s, 0, LO], first[s][0])
        else:
            got(("A-", s))
            summed[3, s, HI] = total(summed[3, s, HI], relay2[s, 1]).astype(jnp.bfloat16)
            remote(("R-", s), summed.at[3, s, HI], final2.at[s, 1, HI], first[s][1])

    out_copies = []

    def finish(s):
        got(("b+", 0, s), ("b-", 0, s), ("r+", 0, s), ("r-", 0, s))
        got(("B+", s), ("B-", s), ("R+", s), ("R-", s))
        at = pl.ds(s * half, half)
        result[at] = total(
            part[0, s, 0], final[0, s, 0], final[0, s, 1], final2[s, 0], final2[s, 1]
        ).astype(jnp.bfloat16)
        out_copies.append(local(result.at[at], out.at[at]))

    def make_shares():
        for made in own_in + small_in:
            made.wait()
        toks = 2 * half
        contract = (((1,), (1,)), ((), ()))
        logits = jnp.concatenate(
            [
                lax.dot_general(w_router[...], own[s], contract, preferred_element_type=jnp.float32)
                for s in range(2)
            ]
            + [jnp.zeros((n_exp, 128 - toks), jnp.float32)],
            axis=1,
        )
        sigmas = jax.nn.sigmoid(logits)
        experts = lax.broadcasted_iota(jnp.int32, (n_exp, 128), 0)
        slots = prio_v.shape[1]
        slot_at = lax.broadcasted_iota(jnp.int32, (slots, 128), 0)
        slot_of = lax.broadcasted_iota(jnp.int32, (slots, 128), 1) * SIDE
        order = jnp.broadcast_to(prio_v[...].astype(jnp.float32), (8, slots)).astype(jnp.bfloat16)
        prior = jnp.full((n_exp, 128), FAR, jnp.float32)
        picked = jnp.zeros((n_exp, 128), jnp.float32)
        for k in range(route_v.shape[0]):
            chosen = jnp.concatenate(
                [route_v[k : k + 1, :], jnp.full((1, 128 - toks), -1, jnp.int32)], axis=1
            )
            hit = chosen == experts
            select = jnp.where(slot_at == slot_of + k, 1.0, 0.0).astype(jnp.bfloat16)
            place = jnp.dot(order, select, preferred_element_type=jnp.float32)[:1]
            prior = jnp.where(hit, place, prior)
            picked = jnp.where(hit, sigmas, picked)
        weights = picked / jnp.sum(picked, axis=0, keepdims=True)
        prior_t = jnp.transpose(
            jnp.concatenate([prior, jnp.full((128 - n_exp, 128), FAR, jnp.float32)], axis=0)
        )[:toks]
        rank_rows = []
        for e in range(n_exp):
            before = prior_t[:, e : e + 1] < prior[e : e + 1, :]
            rank_rows.append(jnp.sum(jnp.where(before, 1.0, 0.0), axis=0, keepdims=True))
        ranks = jnp.concatenate(rank_rows, axis=0)
        hot = (experts == hot_s[0]) | (experts == hot_s[1])
        token_at = lax.broadcasted_iota(jnp.int32, (n_exp, 128), 1)
        keep = (hot | (ranks < capacity)) & (token_at < toks)
        kept = jnp.where(keep, weights, 0.0)
        shares[0, 0] = kept[:8] + pltpu.roll(kept[8:], 64, axis=1)

    run = {
        "O": own_first, "S": spread, "f": pass_first, "g": pass_second, "X": share_x, "Y": share_y,
        "E": expert, "a": far_halves, "b": near_halves, "r": add_second, "F": fold, "A": far_first,
        "B": near_first, "R": add_first, "Z": finish,
    }
    heavy_in = []
    for at, step in enumerate(ORDER):
        if at == 4:
            pl.semaphore_signal(
                far_sem.at[0], inc=1, device_id={"expert": x_plus}, device_id_type=MESH
            )
            pl.semaphore_signal(
                far_sem.at[1], inc=1, device_id={"expert": y_plus}, device_id_type=MESH
            )
            heavy_in += [
                local(tokens.at[pl.ds(s * half, half)], grid_tok.at[0, s, 0]) for s in range(2)
            ]
            heavy_in += [
                local(gate.at[0], w_gate), local(up.at[0], w_up), local(down.at[0], w_down)
            ]
        run[step[0]](*step[1:])
    assert len(landed) == len(copies)
    for made in copies.values():
        made.wait_send()
    for made in out_copies:
        made.wait()


def shards(tokens, router_weight, gate_weight, up_weight, down_weight, routing, priority, hot_list):
    toks, width = tokens.shape
    half = toks // 2
    n_ff = gate_weight.shape[2]
    bf16, f32 = jnp.bfloat16, jnp.float32
    hbm = pl.BlockSpec(memory_space=pltpu.HBM)
    return pl.pallas_call(
        kernel,
        out_shape=jax.ShapeDtypeStruct((toks, width), bf16),
        in_specs=[hbm] * 8,
        out_specs=hbm,
        scratch_shapes=[
            pltpu.VMEM((SIDE, 2, SIDE, half, width), bf16),
            pltpu.VMEM((SIDE, 2, SIDE, half, width), bf16),
            pltpu.VMEM((SIDE, 2, 2, half // 2, width), bf16),
            pltpu.VMEM((SIDE, 2, 2, half, width), bf16),
            pltpu.VMEM((SIDE, 2, half, width), bf16),
            pltpu.VMEM((2, 2, half // 2, width), bf16),
            pltpu.VMEM((2, 2, half, width), bf16),
            pltpu.VMEM((SIDE, SIDE, 8, 128), f32),
            pltpu.VMEM((SIDE * half, 128), f32),
            pltpu.VMEM((width, n_ff), bf16),
            pltpu.VMEM((width, n_ff), bf16),
            pltpu.VMEM((n_ff, width), bf16),
            pltpu.VMEM(router_weight.shape[::-1], bf16),
            pltpu.VMEM((2, half, width), bf16),
            pltpu.VMEM((SIDE * half, n_ff), bf16),
            pltpu.VMEM((toks, width), bf16),
            pltpu.VMEM(routing.shape[::-1], jnp.int32),
            pltpu.VMEM(priority.shape, jnp.int32),
            pltpu.SMEM(hot_list.shape, jnp.int32),
            pltpu.SemaphoreType.DMA((N_SEMS,)),
            pltpu.SemaphoreType.DMA((N_SEMS,)),
            pltpu.SemaphoreType.DMA((16,)),
            pltpu.SemaphoreType.REGULAR((2,)),
        ],
        compiler_params=pltpu.CompilerParams(
            collective_id=0, has_side_effects=True, vmem_limit_bytes=67043328
        ),
    )(
        tokens, router_weight.T, gate_weight, up_weight, down_weight, routing.T, priority, hot_list
    )


def solution(mesh):
    return jax.shard_map(
        shards,
        mesh=mesh,
        in_specs=(
            P(("dp", "expert"), None),
            P(),
            P("expert", None, None),
            P("expert", None, None),
            P("expert", None, None),
            P(("dp", "expert"), None),
            P(("dp", "expert"), None),
            P("dp"),
        ),
        out_specs=P(("dp", "expert"), None),
        check_vma=False,
    )
```

```python
import jax
import jax.numpy as jnp
from jax import lax
from jax.experimental import pallas as pl
from jax.experimental.pallas import tpu as pltpu
from jax.sharding import PartitionSpec as P

MESH = pl.DeviceIdType.MESH
SIDE = 4
LO, HI = pl.ds(0, 16), pl.ds(16, 16)
N_SEMS = 128
FAR = 4096.0
ORDER = (
    ("O", 1), ("O", 0), ("S", 0, 0), ("S", 0, 1), ("X",), ("f", 0, 1), ("f", 0, 0), ("f", 1, 0),
    ("f", 1, 1), ("S", 3, 0), ("S", 3, 1), ("g", 1, 0, 0), ("g", 0, 0, 0), ("g", 0, 0, 1),
    ("g", 1, 0, 1), ("Y",), ("S", 2, 1), ("S", 2, 0), ("g", 0, 3, 1), ("g", 1, 3, 1), ("g", 0, 3, 0),
    ("g", 1, 3, 0), ("S", 1, 1), ("S", 1, 0), ("E", 0, 0), ("E", 0, 1), ("g", 1, 2, 1), ("g", 1, 2, 0),
    ("g", 0, 2, 1), ("g", 0, 2, 0), ("E", 3, 1), ("b", 0, 1), ("b", 0, 0), ("E", 3, 0), ("b", 3, 1),
    ("a", 3, 0), ("g", 0, 1, 1), ("g", 1, 1, 1), ("g", 0, 1, 0), ("g", 1, 1, 0), ("E", 2, 1),
    ("b", 2, 1), ("E", 2, 0), ("b", 2, 0), ("a", 2, 0), ("a", 2, 1), ("r", 0, 3, 0), ("a", 3, 1),
    ("r", 1, 3, 0), ("E", 1, 1), ("a", 1, 1), ("E", 1, 0), ("a", 1, 0), ("b", 3, 0), ("r", 0, 2, 1),
    ("r", 1, 2, 1), ("b", 1, 1), ("r", 0, 2, 0), ("r", 1, 2, 0), ("r", 0, 3, 1), ("r", 1, 3, 1),
    ("b", 1, 0), ("r", 0, 1, 1), ("r", 1, 1, 1), ("r", 0, 1, 0), ("r", 1, 1, 0), ("F", 2, 1), ("A", 1),
    ("F", 3, 0), ("a", 0, 1), ("F", 2, 0), ("A", 0), ("a", 0, 0), ("F", 3, 1), ("B", 0, 0), ("B", 0, 1),
    ("F", 1, 1), ("B", 1, 1), ("F", 1, 0), ("B", 1, 0), ("r", 0, 0, 1), ("r", 1, 0, 1), ("R", 0, 1),
    ("R", 1, 1), ("R", 0, 0), ("R", 1, 0), ("r", 0, 0, 0), ("r", 1, 0, 0), ("Z", 1), ("Z", 0),
)


def kernel(
    tokens, router, gate, up, down, routing, priority, hot_list, out,
    grid_tok, part, relay, final, summed, relay2, final2, shares, columns,
    w_gate, w_up, w_down, w_router, own, hidden, route_v, prio_v, hot_s,
    send_sem, recv_sem, local_sem, far_sem,
):
    me = lax.axis_index("expert")
    my_y, my_x = me // SIDE, me % SIDE
    x_plus = my_y * SIDE + (my_x + 1) % SIDE
    x_minus = my_y * SIDE + (my_x + SIDE - 1) % SIDE
    y_plus = ((my_y + 1) % SIDE) * SIDE + my_x
    y_minus = ((my_y + SIDE - 1) % SIDE) * SIDE + my_x
    x_far = my_y * SIDE + (my_x + 2) % SIDE
    y_far = ((my_y + 2) % SIDE) * SIDE + my_x
    first = ((x_plus, x_minus), (y_plus, y_minus))
    second = ((y_plus, y_minus), (x_plus, x_minus))
    half = own.shape[1]
    n_ff = w_gate.shape[1]
    width = w_gate.shape[0]
    n_exp = SIDE * SIDE
    capacity = min(2 * half, 3 * prio_v.shape[1] // (2 * n_exp))

    copies, landed = {}, set()

    def remote(key, src, dst, device):
        index = len(copies)
        copies[key] = pltpu.make_async_remote_copy(
            src_ref=src, dst_ref=dst, send_sem=send_sem.at[index], recv_sem=recv_sem.at[index],
            device_id={"expert": device}, device_id_type=MESH,
        )
        copies[key].start()

    def got(*keys):
        for key in keys:
            if key not in landed:
                landed.add(key)
                copies[key].wait_recv()

    local_count = [0]

    def local(src, dst):
        made = pltpu.make_async_copy(src, dst, local_sem.at[local_count[0]])
        local_count[0] += 1
        made.start()
        return made

    barrier = pltpu.get_barrier_semaphore()
    for device in (x_plus, x_minus, y_plus, y_minus):
        pl.semaphore_signal(barrier, inc=1, device_id={"expert": device}, device_id_type=MESH)
    own_in = [local(tokens.at[pl.ds(s * half, half)], own.at[s]) for s in range(2)]
    small_in = [
        local(routing, route_v), local(priority, prio_v), local(hot_list, hot_s), local(router, w_router)
    ]
    pl.semaphore_wait(barrier, 4)

    def own_first(s):
        mine = tokens.at[pl.ds(s * half, half)]
        remote(("O+", s), mine, grid_tok.at[3, s, 0], first[s][0])
        remote(("O-", s), mine, grid_tok.at[1, s, 0], first[s][1])

    def spread(d, s):
        if d == 0:
            mine = tokens.at[pl.ds(s * half, half)]
        else:
            got(*{3: [("O+", s)], 1: [("O-", s)], 2: [("f+", s), ("f-", s)]}[d])
            mine = grid_tok.at[d, s, 0]
        remote(("S+", d, s), mine, grid_tok.at[d, s, 3], second[s][0])
        remote(("S-", d, s), mine, grid_tok.at[d, s, 1], second[s][1])

    def pass_first(plus, s):
        if plus:
            got(("O+", s))
            remote(("f+", s), grid_tok.at[3, s, 0, LO], grid_tok.at[2, s, 0, LO], first[s][0])
        else:
            got(("O-", s))
            remote(("f-", s), grid_tok.at[1, s, 0, HI], grid_tok.at[2, s, 0, HI], first[s][1])

    def pass_second(plus, d, s):
        if plus:
            got(("S+", d, s))
            remote(("g+", d, s), grid_tok.at[d, s, 3, LO], grid_tok.at[d, s, 2, LO], second[s][0])
        else:
            got(("S-", d, s))
            remote(("g-", d, s), grid_tok.at[d, s, 1, HI], grid_tok.at[d, s, 2, HI], second[s][1])

    def share_x():
        make_shares()
        pl.semaphore_wait(far_sem.at[0], 1)
        remote("X+", shares.at[0, 0], shares.at[3, 0], x_plus)
        remote("X-", shares.at[0, 0], shares.at[1, 0], x_minus)
        remote("X2", shares.at[0, 0], shares.at[2, 0], x_far)

    def share_y():
        got("X+", "X-", "X2")
        pl.semaphore_wait(far_sem.at[1], 1)
        remote("Y+", shares.at[:, 0], shares.at[:, 3], y_plus)
        remote("Y-", shares.at[:, 0], shares.at[:, 1], y_minus)
        remote("Y2", shares.at[:, 0], shares.at[:, 2], y_far)

    my_row, my_half = me % 8, me // 8
    rows = SIDE * half
    loaded = []

    def expert(d, s):
        if not loaded:
            got("X+", "X-", "X2", "Y+", "Y-", "Y2")
            for made in heavy_in:
                made.wait()
            loaded.append(1)
        got(("S+", d, s), ("S-", d, s), ("g+", d, s), ("g-", d, s))
        got(*{0: [], 3: [("O+", s)], 1: [("O-", s)], 2: [("f+", s), ("f-", s)]}[d])
        share_row = lax.broadcasted_iota(jnp.int32, (8, 128), 0) == my_row
        token_lane = lax.broadcasted_iota(jnp.int32, (half, 128), 1)
        token_row = lax.broadcasted_iota(jnp.int32, (half, 128), 0)
        pick = token_lane == token_row + (my_half * 64 + s * half)
        for e in range(SIDE):
            held = shares[d, e] if s == 0 else shares[e, d]
            row = jnp.sum(jnp.where(share_row, held, 0.0), axis=0, keepdims=True)
            row = jnp.broadcast_to(row, (half, 128))
            columns[pl.ds(e * half, half)] = jnp.broadcast_to(
                jnp.sum(jnp.where(pick, row, 0.0), axis=1, keepdims=True), (half, 128)
            )
        for n in range(n_ff // 256):
            at = pl.ds(n * 256, 256)
            block = grid_tok[d, s].reshape(rows, width)
            g = jnp.dot(block, w_gate[:, at], preferred_element_type=jnp.float32)
            u = jnp.dot(block, w_up[:, at], preferred_element_type=jnp.float32)
            hidden[:, at] = (g / (1.0 + jnp.exp(-g)) * u).astype(jnp.bfloat16)
        for n in range(width // 256):
            at = pl.ds(n * 256, 256)
            o = jnp.dot(hidden[...], w_down[:, at], preferred_element_type=jnp.float32)
            scale = jnp.concatenate([columns[...], columns[...]], axis=1)
            part[d, s, :, :, at] = (o * scale).astype(jnp.bfloat16).reshape(SIDE, half, 256)

    def total(*values):
        result = values[0].astype(jnp.float32)
        for value in values[1:]:
            result = result + value.astype(jnp.float32)
        return result

    def far_halves(d, s):
        remote(("a+", d, s), part.at[d, s, 2, LO], relay.at[d, s, 0], second[s][0])
        remote(("a-", d, s), part.at[d, s, 2, HI], relay.at[d, s, 1], second[s][1])

    def near_halves(d, s):
        remote(("b+", d, s), part.at[d, s, 1, HI], final.at[d, s, 0, HI], second[s][0])
        remote(("b-", d, s), part.at[d, s, 3, LO], final.at[d, s, 1, LO], second[s][1])

    def add_second(plus, d, s):
        if plus:
            got(("a+", d, s))
            part[d, s, 1, LO] = total(part[d, s, 1, LO], relay[d, s, 0]).astype(jnp.bfloat16)
            remote(("r+", d, s), part.at[d, s, 1, LO], final.at[d, s, 0, LO], second[s][0])
        else:
            got(("a-", d, s))
            part[d, s, 3, HI] = total(part[d, s, 3, HI], relay[d, s, 1]).astype(jnp.bfloat16)
            remote(("r-", d, s), part.at[d, s, 3, HI], final.at[d, s, 1, HI], second[s][1])

    def fold(d, s):
        got(("b+", d, s), ("b-", d, s), ("r+", d, s), ("r-", d, s))
        summed[d, s] = total(part[d, s, 0], final[d, s, 0], final[d, s, 1]).astype(jnp.bfloat16)

    def far_first(s):
        remote(("A+", s), summed.at[2, s, LO], relay2.at[s, 0], first[s][0])
        remote(("A-", s), summed.at[2, s, HI], relay2.at[s, 1], first[s][1])

    def near_first(plus, s):
        if plus:
            remote(("B+", s), summed.at[1, s, HI], final2.at[s, 0, HI], first[s][0])
        else:
            remote(("B-", s), summed.at[3, s, LO], final2.at[s, 1, LO], first[s][1])

    def add_first(plus, s):
        if plus:
            got(("A+", s))
            summed[1, s, LO] = total(summed[1, s, LO], relay2[s, 0]).astype(jnp.bfloat16)
            remote(("R+", s), summed.at[1, s, LO], final2.at[s, 0, LO], first[s][0])
        else:
            got(("A-", s))
            summed[3, s, HI] = total(summed[3, s, HI], relay2[s, 1]).astype(jnp.bfloat16)
            remote(("R-", s), summed.at[3, s, HI], final2.at[s, 1, HI], first[s][1])

    def finish(s):
        got(("b+", 0, s), ("b-", 0, s), ("r+", 0, s), ("r-", 0, s))
        got(("B+", s), ("B-", s), ("R+", s), ("R-", s))
        at = pl.ds(s * half, half)
        out[at] = total(
            part[0, s, 0], final[0, s, 0], final[0, s, 1], final2[s, 0], final2[s, 1]
        ).astype(jnp.bfloat16)

    def make_shares():
        for made in own_in + small_in:
            made.wait()
        toks = 2 * half
        contract = (((1,), (1,)), ((), ()))
        logits = jnp.concatenate(
            [
                lax.dot_general(w_router[...], own[s], contract, preferred_element_type=jnp.float32)
                for s in range(2)
            ]
            + [jnp.zeros((n_exp, 128 - toks), jnp.float32)],
            axis=1,
        )
        sigmas = jax.nn.sigmoid(logits)
        experts = lax.broadcasted_iota(jnp.int32, (n_exp, 128), 0)
        slots = prio_v.shape[1]
        slot_at = lax.broadcasted_iota(jnp.int32, (slots, 128), 0)
        slot_of = lax.broadcasted_iota(jnp.int32, (slots, 128), 1) * SIDE
        order = jnp.broadcast_to(prio_v[...].astype(jnp.float32), (8, slots)).astype(jnp.bfloat16)
        prior = jnp.full((n_exp, 128), FAR, jnp.float32)
        picked = jnp.zeros((n_exp, 128), jnp.float32)
        for k in range(route_v.shape[0]):
            chosen = jnp.concatenate(
                [route_v[k : k + 1, :], jnp.full((1, 128 - toks), -1, jnp.int32)], axis=1
            )
            hit = chosen == experts
            select = jnp.where(slot_at == slot_of + k, 1.0, 0.0).astype(jnp.bfloat16)
            place = jnp.dot(order, select, preferred_element_type=jnp.float32)[:1]
            prior = jnp.where(hit, place, prior)
            picked = jnp.where(hit, sigmas, picked)
        weights = picked / jnp.sum(picked, axis=0, keepdims=True)
        prior_t = jnp.transpose(
            jnp.concatenate([prior, jnp.full((128 - n_exp, 128), FAR, jnp.float32)], axis=0)
        )[:toks]
        rank_rows = []
        for e in range(n_exp):
            before = prior_t[:, e : e + 1] < prior[e : e + 1, :]
            rank_rows.append(jnp.sum(jnp.where(before, 1.0, 0.0), axis=0, keepdims=True))
        ranks = jnp.concatenate(rank_rows, axis=0)
        hot = (experts == hot_s[0]) | (experts == hot_s[1])
        token_at = lax.broadcasted_iota(jnp.int32, (n_exp, 128), 1)
        keep = (hot | (ranks < capacity)) & (token_at < toks)
        kept = jnp.where(keep, weights, 0.0)
        shares[0, 0] = kept[:8] + pltpu.roll(kept[8:], 64, axis=1)

    run = {
        "O": own_first, "S": spread, "f": pass_first, "g": pass_second, "X": share_x, "Y": share_y,
        "E": expert, "a": far_halves, "b": near_halves, "r": add_second, "F": fold, "A": far_first,
        "B": near_first, "R": add_first, "Z": finish,
    }
    heavy_in = []
    for at, step in enumerate(ORDER):
        if at == 4:
            pl.semaphore_signal(
                far_sem.at[0], inc=1, device_id={"expert": x_plus}, device_id_type=MESH
            )
            pl.semaphore_signal(
                far_sem.at[1], inc=1, device_id={"expert": y_plus}, device_id_type=MESH
            )
            heavy_in += [
                local(tokens.at[pl.ds(s * half, half)], grid_tok.at[0, s, 0]) for s in range(2)
            ]
            heavy_in += [
                local(gate.at[0], w_gate), local(up.at[0], w_up), local(down.at[0], w_down)
            ]
        run[step[0]](*step[1:])
    assert len(landed) == len(copies)
    for made in copies.values():
        made.wait_send()


def shards(tokens, router_weight, gate_weight, up_weight, down_weight, routing, priority, hot_list):
    toks, width = tokens.shape
    half = toks // 2
    n_ff = gate_weight.shape[2]
    bf16, f32 = jnp.bfloat16, jnp.float32
    hbm = pl.BlockSpec(memory_space=pltpu.HBM)
    return pl.pallas_call(
        kernel,
        out_shape=jax.ShapeDtypeStruct((toks, width), bf16),
        in_specs=[hbm] * 8,
        out_specs=pl.BlockSpec(memory_space=pltpu.VMEM),
        scratch_shapes=[
            pltpu.VMEM((SIDE, 2, SIDE, half, width), bf16),
            pltpu.VMEM((SIDE, 2, SIDE, half, width), bf16),
            pltpu.VMEM((SIDE, 2, 2, half // 2, width), bf16),
            pltpu.VMEM((SIDE, 2, 2, half, width), bf16),
            pltpu.VMEM((SIDE, 2, half, width), bf16),
            pltpu.VMEM((2, 2, half // 2, width), bf16),
            pltpu.VMEM((2, 2, half, width), bf16),
            pltpu.VMEM((SIDE, SIDE, 8, 128), f32),
            pltpu.VMEM((SIDE * half, 128), f32),
            pltpu.VMEM((width, n_ff), bf16),
            pltpu.VMEM((width, n_ff), bf16),
            pltpu.VMEM((n_ff, width), bf16),
            pltpu.VMEM(router_weight.shape[::-1], bf16),
            pltpu.VMEM((2, half, width), bf16),
            pltpu.VMEM((SIDE * half, n_ff), bf16),
            pltpu.VMEM(routing.shape[::-1], jnp.int32),
            pltpu.VMEM(priority.shape, jnp.int32),
            pltpu.SMEM(hot_list.shape, jnp.int32),
            pltpu.SemaphoreType.DMA((N_SEMS,)),
            pltpu.SemaphoreType.DMA((N_SEMS,)),
            pltpu.SemaphoreType.DMA((16,)),
            pltpu.SemaphoreType.REGULAR((2,)),
        ],
        compiler_params=pltpu.CompilerParams(
            collective_id=0, has_side_effects=True, vmem_limit_bytes=51683328
        ),
    )(*(pltpu.with_memory_space_constraint(v, pltpu.HBM) for v in (
        tokens, router_weight.T, gate_weight, up_weight, down_weight, routing.T, priority, hot_list
    )))


def solution(mesh):
    return jax.shard_map(
        shards,
        mesh=mesh,
        in_specs=(
            P(("dp", "expert"), None),
            P(),
            P("expert", None, None),
            P("expert", None, None),
            P("expert", None, None),
            P(("dp", "expert"), None),
            P(("dp", "expert"), None),
            P("dp"),
        ),
        out_specs=P(("dp", "expert"), None),
        check_vma=False,
    )
```

```python
import jax
import jax.numpy as jnp
from jax import lax
from jax.experimental import pallas as pl
from jax.experimental.pallas import tpu as pltpu
from jax.sharding import PartitionSpec as P

MESH = pl.DeviceIdType.MESH
SIDE = 4
LO, HI = pl.ds(0, 16), pl.ds(16, 16)
N_SEMS = 128
FAR = 4096.0
ORDER = (
    ("O", 0), ("O", 1), ("S", 0, 1), ("S", 0, 0), ("f", 0, 0), ("f", 1, 0), ("f", 1, 1), ("f", 0, 1),
    ("S", 1, 1), ("S", 1, 0), ("X",), ("S", 2, 0), ("S", 2, 1), ("g", 1, 1, 0), ("g", 0, 1, 0),
    ("S", 3, 1), ("Y",), ("g", 1, 1, 1), ("g", 0, 1, 1), ("S", 3, 0), ("g", 0, 0, 0), ("g", 0, 2, 1),
    ("g", 1, 2, 0), ("g", 1, 2, 1), ("g", 0, 2, 0), ("g", 1, 0, 0), ("g", 0, 3, 1), ("g", 1, 3, 1),
    ("E", 1, 0), ("g", 1, 0, 1), ("g", 0, 0, 1), ("b", 1, 0), ("E", 1, 1), ("b", 1, 1), ("g", 0, 3, 0),
    ("a", 1, 0), ("E", 2, 1), ("g", 1, 3, 0), ("a", 2, 1), ("E", 2, 0), ("a", 1, 1), ("a", 2, 0),
    ("b", 2, 0), ("E", 3, 1), ("a", 3, 1), ("b", 3, 1), ("r", 1, 2, 1), ("r", 1, 1, 0), ("r", 0, 1, 0),
    ("b", 2, 1), ("r", 0, 2, 1), ("E", 3, 0), ("r", 1, 1, 1), ("a", 3, 0), ("r", 0, 2, 0),
    ("r", 0, 1, 1), ("r", 1, 2, 0), ("E", 0, 0), ("E", 0, 1), ("a", 0, 0), ("r", 0, 3, 1), ("a", 0, 1),
    ("b", 3, 0), ("r", 0, 3, 0), ("F", 1, 0), ("r", 1, 3, 0), ("F", 2, 1), ("r", 1, 3, 1), ("A", 1),
    ("F", 2, 0), ("A", 0), ("B", 1, 0), ("r", 0, 0, 0), ("b", 0, 1), ("F", 1, 1), ("b", 0, 0),
    ("r", 0, 0, 1), ("F", 3, 1), ("B", 1, 1), ("F", 3, 0), ("r", 1, 0, 1), ("r", 1, 0, 0), ("R", 0, 0),
    ("B", 0, 1), ("B", 0, 0), ("R", 1, 1), ("R", 1, 0), ("R", 0, 1), ("P", 1), ("P", 0), ("Z", 0),
    ("Z", 1),
)


def kernel(
    tokens, router, gate, up, down, routing, priority, hot_list, out,
    grid_tok, part, relay, final, summed, relay2, final2, shares, columns,
    w_gate, w_up, w_down, w_router, own, mine, hidden, route_v, prio_v, hot_s,
    send_sem, recv_sem, local_sem, far_sem,
):
    me = lax.axis_index("expert")
    my_y, my_x = me // SIDE, me % SIDE
    x_plus = my_y * SIDE + (my_x + 1) % SIDE
    x_minus = my_y * SIDE + (my_x + SIDE - 1) % SIDE
    y_plus = ((my_y + 1) % SIDE) * SIDE + my_x
    y_minus = ((my_y + SIDE - 1) % SIDE) * SIDE + my_x
    x_far = my_y * SIDE + (my_x + 2) % SIDE
    y_far = ((my_y + 2) % SIDE) * SIDE + my_x
    first = ((x_plus, x_minus), (y_plus, y_minus))
    second = ((y_plus, y_minus), (x_plus, x_minus))
    half = own.shape[1]
    n_ff = w_gate.shape[1]
    width = w_gate.shape[0]
    n_exp = SIDE * SIDE
    capacity = min(2 * half, 3 * prio_v.shape[1] // (2 * n_exp))

    copies, landed = {}, set()

    def remote(key, src, dst, device):
        index = len(copies)
        copies[key] = pltpu.make_async_remote_copy(
            src_ref=src, dst_ref=dst, send_sem=send_sem.at[index], recv_sem=recv_sem.at[index],
            device_id={"expert": device}, device_id_type=MESH,
        )
        copies[key].start()

    def got(*keys):
        for key in keys:
            if key not in landed:
                landed.add(key)
                copies[key].wait_recv()

    local_count = [0]

    def local(src, dst):
        made = pltpu.make_async_copy(src, dst, local_sem.at[local_count[0]])
        local_count[0] += 1
        made.start()
        return made

    barrier = pltpu.get_barrier_semaphore()
    for device in (x_plus, x_minus, y_plus, y_minus):
        pl.semaphore_signal(barrier, inc=1, device_id={"expert": device}, device_id_type=MESH)
    own_in = [local(tokens.at[pl.ds(s * half, half)], own.at[s]) for s in range(2)]
    small_in = [
        local(routing, route_v), local(priority, prio_v), local(hot_list, hot_s), local(router, w_router)
    ]
    pl.semaphore_wait(barrier, 4)

    def settle(left, keep):
        while len(left) > keep:
            left.pop(0).wait_send()

    def own_first(s):
        block = tokens.at[pl.ds(s * half, half)]
        remote(("O+", s), block, grid_tok.at[3, s, 0], first[s][0])
        remote(("O-", s), block, grid_tok.at[1, s, 0], first[s][1])

    def spread(d, s):
        if d == 0:
            block = tokens.at[pl.ds(s * half, half)]
        else:
            got(*{3: [("O+", s)], 1: [("O-", s)], 2: [("f+", s), ("f-", s)]}[d])
            block = grid_tok.at[d, s, 0]
        remote(("S+", d, s), block, grid_tok.at[d, s, 3], second[s][0])
        remote(("S-", d, s), block, grid_tok.at[d, s, 1], second[s][1])

    def pass_first(plus, s):
        if plus:
            got(("O+", s))
            remote(("f+", s), grid_tok.at[3, s, 0, LO], grid_tok.at[2, s, 0, LO], first[s][0])
        else:
            got(("O-", s))
            remote(("f-", s), grid_tok.at[1, s, 0, HI], grid_tok.at[2, s, 0, HI], first[s][1])

    def pass_second(plus, d, s):
        if plus:
            got(("S+", d, s))
            remote(("g+", d, s), grid_tok.at[d, s, 3, LO], grid_tok.at[d, s, 2, LO], second[s][0])
        else:
            got(("S-", d, s))
            remote(("g-", d, s), grid_tok.at[d, s, 1, HI], grid_tok.at[d, s, 2, HI], second[s][1])

    def share_x():
        make_shares()
        pl.semaphore_wait(far_sem.at[0], 1)
        remote("X+", shares.at[0, 0], shares.at[3, 0], x_plus)
        remote("X-", shares.at[0, 0], shares.at[1, 0], x_minus)
        remote("X2", shares.at[0, 0], shares.at[2, 0], x_far)

    def share_y():
        got("X+", "X-", "X2")
        pl.semaphore_wait(far_sem.at[1], 1)
        remote("Y+", shares.at[:, 0], shares.at[:, 3], y_plus)
        remote("Y-", shares.at[:, 0], shares.at[:, 1], y_minus)
        remote("Y2", shares.at[:, 0], shares.at[:, 2], y_far)

    my_row, my_half = me % 8, me // 8
    rows = SIDE * half
    loaded = []

    def expert(d, s):
        if not loaded:
            got("X+", "X-", "X2", "Y+", "Y-", "Y2")
            for made in heavy_in:
                made.wait()
            loaded.append(1)
        got(("S+", d, s), ("S-", d, s), ("g+", d, s), ("g-", d, s))
        got(*{0: [], 3: [("O+", s)], 1: [("O-", s)], 2: [("f+", s), ("f-", s)]}[d])
        share_row = lax.broadcasted_iota(jnp.int32, (8, 128), 0) == my_row
        token_lane = lax.broadcasted_iota(jnp.int32, (half, 128), 1)
        token_row = lax.broadcasted_iota(jnp.int32, (half, 128), 0)
        pick = token_lane == token_row + (my_half * 64 + s * half)
        for e in range(SIDE):
            held = shares[d, e] if s == 0 else shares[e, d]
            row = jnp.sum(jnp.where(share_row, held, 0.0), axis=0, keepdims=True)
            row = jnp.broadcast_to(row, (half, 128))
            columns[pl.ds(e * half, half)] = jnp.broadcast_to(
                jnp.sum(jnp.where(pick, row, 0.0), axis=1, keepdims=True), (half, 128)
            )
        for n in range(n_ff // 256):
            at = pl.ds(n * 256, 256)
            block = grid_tok[d, s].reshape(rows, width)
            g = jnp.dot(block, w_gate[:, at], preferred_element_type=jnp.float32)
            u = jnp.dot(block, w_up[:, at], preferred_element_type=jnp.float32)
            hidden[:, at] = (g / (1.0 + jnp.exp(-g)) * u).astype(jnp.bfloat16)
        for n in range(width // 256):
            at = pl.ds(n * 256, 256)
            o = jnp.dot(hidden[...], w_down[:, at], preferred_element_type=jnp.float32)
            scale = jnp.concatenate([columns[...], columns[...]], axis=1)
            part[d, s, :, :, at] = (o * scale).astype(jnp.bfloat16).reshape(SIDE, half, 256)

    def total(*values):
        result = values[0].astype(jnp.float32)
        for value in values[1:]:
            result = result + value.astype(jnp.float32)
        return result

    def far_halves(d, s):
        remote(("a+", d, s), part.at[d, s, 2, LO], relay.at[d, s, 0], second[s][0])
        remote(("a-", d, s), part.at[d, s, 2, HI], relay.at[d, s, 1], second[s][1])

    def near_halves(d, s):
        remote(("b+", d, s), part.at[d, s, 1, HI], final.at[d, s, 0, HI], second[s][0])
        remote(("b-", d, s), part.at[d, s, 3, LO], final.at[d, s, 1, LO], second[s][1])

    def add_second(plus, d, s):
        if plus:
            got(("a+", d, s))
            part[d, s, 1, LO] = total(part[d, s, 1, LO], relay[d, s, 0]).astype(jnp.bfloat16)
            remote(("r+", d, s), part.at[d, s, 1, LO], final.at[d, s, 0, LO], second[s][0])
        else:
            got(("a-", d, s))
            part[d, s, 3, HI] = total(part[d, s, 3, HI], relay[d, s, 1]).astype(jnp.bfloat16)
            remote(("r-", d, s), part.at[d, s, 3, HI], final.at[d, s, 1, HI], second[s][1])

    def fold(d, s):
        got(("b+", d, s), ("b-", d, s), ("r+", d, s), ("r-", d, s))
        summed[d, s] = total(part[d, s, 0], final[d, s, 0], final[d, s, 1]).astype(jnp.bfloat16)

    def far_first(s):
        remote(("A+", s), summed.at[2, s, LO], relay2.at[s, 0], first[s][0])
        remote(("A-", s), summed.at[2, s, HI], relay2.at[s, 1], first[s][1])

    def near_first(plus, s):
        if plus:
            remote(("B+", s), summed.at[1, s, HI], final2.at[s, 0, HI], first[s][0])
        else:
            remote(("B-", s), summed.at[3, s, LO], final2.at[s, 1, LO], first[s][1])

    def add_first(plus, s):
        if plus:
            got(("A+", s))
            summed[1, s, LO] = total(summed[1, s, LO], relay2[s, 0]).astype(jnp.bfloat16)
            remote(("R+", s), summed.at[1, s, LO], final2.at[s, 0, LO], first[s][0])
        else:
            got(("A-", s))
            summed[3, s, HI] = total(summed[3, s, HI], relay2[s, 1]).astype(jnp.bfloat16)
            remote(("R-", s), summed.at[3, s, HI], final2.at[s, 1, HI], first[s][1])

    def fold_own(s):
        got(("b+", 0, s), ("b-", 0, s), ("r+", 0, s), ("r-", 0, s))
        mine[s] = total(part[0, s, 0], final[0, s, 0], final[0, s, 1])

    def finish(s):
        got(("B+", s), ("B-", s), ("R+", s), ("R-", s))
        out[pl.ds(s * half, half)] = total(mine[s], final2[s, 0], final2[s, 1]).astype(jnp.bfloat16)

    def make_shares():
        for made in own_in + small_in:
            made.wait()
        toks = 2 * half
        contract = (((1,), (1,)), ((), ()))
        logits = jnp.concatenate(
            [
                lax.dot_general(w_router[...], own[s], contract, preferred_element_type=jnp.float32)
                for s in range(2)
            ]
            + [jnp.zeros((n_exp, 128 - toks), jnp.float32)],
            axis=1,
        )
        sigmas = jax.nn.sigmoid(logits)
        experts = lax.broadcasted_iota(jnp.int32, (n_exp, 128), 0)
        slots = prio_v.shape[1]
        slot_at = lax.broadcasted_iota(jnp.int32, (slots, 128), 0)
        slot_of = lax.broadcasted_iota(jnp.int32, (slots, 128), 1) * SIDE
        order = jnp.broadcast_to(prio_v[...].astype(jnp.float32), (8, slots)).astype(jnp.bfloat16)
        prior = jnp.full((n_exp, 128), FAR, jnp.float32)
        picked = jnp.zeros((n_exp, 128), jnp.float32)
        for k in range(route_v.shape[0]):
            chosen = jnp.concatenate(
                [route_v[k : k + 1, :], jnp.full((1, 128 - toks), -1, jnp.int32)], axis=1
            )
            hit = chosen == experts
            select = jnp.where(slot_at == slot_of + k, 1.0, 0.0).astype(jnp.bfloat16)
            place = jnp.dot(order, select, preferred_element_type=jnp.float32)[:1]
            prior = jnp.where(hit, place, prior)
            picked = jnp.where(hit, sigmas, picked)
        weights = picked / jnp.sum(picked, axis=0, keepdims=True)
        prior_t = jnp.transpose(
            jnp.concatenate([prior, jnp.full((128 - n_exp, 128), FAR, jnp.float32)], axis=0)
        )[:toks]
        rank_rows = []
        for e in range(n_exp):
            before = prior_t[:, e : e + 1] < prior[e : e + 1, :]
            rank_rows.append(jnp.sum(jnp.where(before, 1.0, 0.0), axis=0, keepdims=True))
        ranks = jnp.concatenate(rank_rows, axis=0)
        hot = (experts == hot_s[0]) | (experts == hot_s[1])
        token_at = lax.broadcasted_iota(jnp.int32, (n_exp, 128), 1)
        keep = (hot | (ranks < capacity)) & (token_at < toks)
        kept = jnp.where(keep, weights, 0.0)
        shares[0, 0] = kept[:8] + pltpu.roll(kept[8:], 64, axis=1)

    run = {
        "O": own_first, "S": spread, "f": pass_first, "g": pass_second, "X": share_x, "Y": share_y,
        "E": expert, "a": far_halves, "b": near_halves, "r": add_second, "F": fold, "A": far_first,
        "B": near_first, "R": add_first, "P": fold_own, "Z": finish,
    }
    heavy_in, left = [], []
    for at, step in enumerate(ORDER):
        if at == 4:
            pl.semaphore_signal(
                far_sem.at[0], inc=1, device_id={"expert": x_plus}, device_id_type=MESH
            )
            pl.semaphore_signal(
                far_sem.at[1], inc=1, device_id={"expert": y_plus}, device_id_type=MESH
            )
            heavy_in += [
                local(tokens.at[pl.ds(s * half, half)], grid_tok.at[0, s, 0]) for s in range(2)
            ]
            heavy_in += [
                local(gate.at[0], w_gate), local(up.at[0], w_up), local(down.at[0], w_down)
            ]
        before = len(copies)
        if step[0] == "P":
            settle(left, 12)
        run[step[0]](*step[1:])
        left += list(copies.values())[before:]
        settle(left, 40)
    assert len(landed) == len(copies)
    settle(left, 0)


def shards(tokens, router_weight, gate_weight, up_weight, down_weight, routing, priority, hot_list):
    toks, width = tokens.shape
    half = toks // 2
    n_ff = gate_weight.shape[2]
    bf16, f32 = jnp.bfloat16, jnp.float32
    hbm = pl.BlockSpec(memory_space=pltpu.HBM)
    return pl.pallas_call(
        kernel,
        out_shape=jax.ShapeDtypeStruct((toks, width), bf16),
        in_specs=[hbm] * 8,
        out_specs=pl.BlockSpec(memory_space=pltpu.VMEM),
        scratch_shapes=[
            pltpu.VMEM((SIDE, 2, SIDE, half, width), bf16),
            pltpu.VMEM((SIDE, 2, SIDE, half, width), bf16),
            pltpu.VMEM((SIDE, 2, 2, half // 2, width), bf16),
            pltpu.VMEM((SIDE, 2, 2, half, width), bf16),
            pltpu.VMEM((SIDE, 2, half, width), bf16),
            pltpu.VMEM((2, 2, half // 2, width), bf16),
            pltpu.VMEM((2, 2, half, width), bf16),
            pltpu.VMEM((SIDE, SIDE, 8, 128), f32),
            pltpu.VMEM((SIDE * half, 128), f32),
            pltpu.VMEM((width, n_ff), bf16),
            pltpu.VMEM((width, n_ff), bf16),
            pltpu.VMEM((n_ff, width), bf16),
            pltpu.VMEM(router_weight.shape[::-1], bf16),
            pltpu.VMEM((2, half, width), bf16),
            pltpu.VMEM((2, half, width), f32),
            pltpu.VMEM((SIDE * half, n_ff), bf16),
            pltpu.VMEM(routing.shape[::-1], jnp.int32),
            pltpu.VMEM(priority.shape, jnp.int32),
            pltpu.SMEM(hot_list.shape, jnp.int32),
            pltpu.SemaphoreType.DMA((N_SEMS,)),
            pltpu.SemaphoreType.DMA((N_SEMS,)),
            pltpu.SemaphoreType.DMA((16,)),
            pltpu.SemaphoreType.REGULAR((2,)),
        ],
        compiler_params=pltpu.CompilerParams(
            collective_id=0, has_side_effects=True, vmem_limit_bytes=51683328
        ),
    )(*(pltpu.with_memory_space_constraint(v, pltpu.HBM) for v in (
        tokens, router_weight.T, gate_weight, up_weight, down_weight, routing.T, priority, hot_list
    )))


def solution(mesh):
    return jax.shard_map(
        shards,
        mesh=mesh,
        in_specs=(
            P(("dp", "expert"), None),
            P(),
            P("expert", None, None),
            P("expert", None, None),
            P("expert", None, None),
            P(("dp", "expert"), None),
            P(("dp", "expert"), None),
            P("dp"),
        ),
        out_specs=P(("dp", "expert"), None),
        check_vma=False,
    )
```

```python
import jax
import jax.numpy as jnp
from jax import lax
from jax.experimental import pallas as pl
from jax.experimental.pallas import tpu as pltpu
from jax.sharding import PartitionSpec as P

MESH = pl.DeviceIdType.MESH
SIDE = 4
LO, HI = pl.ds(0, 16), pl.ds(16, 16)
N_SEMS = 128
FAR = 4096.0
ORDER = (
    ("O", 0), ("O", 1), ("S", 0, 1), ("S", 0, 0), ("X",), ("S", 3, 0), ("S", 1, 1), ("f", 1, 1),
    ("f", 1, 0), ("f", 0, 0), ("g", 0, 0, 1), ("f", 0, 1), ("Y",), ("g", 1, 0, 1), ("S", 1, 0),
    ("g", 1, 3, 0), ("g", 0, 3, 0), ("g", 0, 1, 1), ("g", 1, 1, 1), ("S", 2, 1), ("S", 3, 1),
    ("S", 2, 0), ("E", 0, 1), ("g", 1, 1, 0), ("g", 1, 0, 0), ("g", 0, 1, 0), ("E", 1, 1),
    ("g", 0, 2, 1), ("g", 1, 2, 1), ("a", 1, 1), ("a", 0, 1), ("g", 0, 0, 0), ("E", 3, 0),
    ("g", 0, 2, 0), ("g", 1, 2, 0), ("a", 3, 0), ("b", 3, 0), ("g", 1, 3, 1), ("b", 1, 1),
    ("g", 0, 3, 1), ("E", 1, 0), ("b", 1, 0), ("a", 1, 0), ("E", 2, 1), ("a", 2, 1), ("b", 2, 1),
    ("E", 2, 0), ("a", 2, 0), ("r", 0, 0, 1), ("r", 1, 1, 1), ("b", 2, 0), ("E", 3, 1), ("a", 3, 1),
    ("r", 1, 3, 0), ("r", 1, 2, 1), ("r", 0, 3, 0), ("r", 1, 0, 1), ("r", 0, 2, 1), ("r", 0, 1, 1),
    ("r", 0, 2, 0), ("r", 1, 2, 0), ("r", 1, 1, 0), ("b", 3, 1), ("r", 0, 1, 0), ("E", 0, 0),
    ("a", 0, 0), ("r", 1, 3, 1), ("r", 0, 3, 1), ("F", 2, 1), ("A", 1), ("F", 2, 0), ("A", 0),
    ("b", 0, 0), ("F", 1, 1), ("F", 3, 0), ("B", 0, 0), ("b", 0, 1), ("B", 1, 1), ("r", 0, 0, 0),
    ("F", 1, 0), ("B", 1, 0), ("r", 1, 0, 0), ("F", 3, 1), ("R", 0, 1), ("R", 1, 1), ("R", 0, 0),
    ("R", 1, 0), ("B", 0, 1), ("P", 1), ("P", 0), ("Z", 0), ("Z", 1),
)


def kernel(
    tokens, router, gate, up, down, routing, priority, hot_list, out,
    grid_tok, part, relay, final, summed, relay2, final2, shares, columns,
    w_gate, w_up, w_down, w_router, own, mine, hidden, route_v, prio_v, hot_s,
    send_sem, recv_sem, local_sem, far_sem,
):
    me = lax.axis_index("expert")
    my_y, my_x = me // SIDE, me % SIDE
    x_plus = my_y * SIDE + (my_x + 1) % SIDE
    x_minus = my_y * SIDE + (my_x + SIDE - 1) % SIDE
    y_plus = ((my_y + 1) % SIDE) * SIDE + my_x
    y_minus = ((my_y + SIDE - 1) % SIDE) * SIDE + my_x
    x_far = my_y * SIDE + (my_x + 2) % SIDE
    y_far = ((my_y + 2) % SIDE) * SIDE + my_x
    first = ((x_plus, x_minus), (y_plus, y_minus))
    second = ((y_plus, y_minus), (x_plus, x_minus))
    half = own.shape[1]
    n_ff = w_gate.shape[1]
    width = w_gate.shape[0]
    n_exp = SIDE * SIDE
    capacity = min(2 * half, 3 * prio_v.shape[1] // (2 * n_exp))

    copies, landed = {}, set()

    def remote(key, src, dst, device):
        index = len(copies)
        copies[key] = pltpu.make_async_remote_copy(
            src_ref=src, dst_ref=dst, send_sem=send_sem.at[index], recv_sem=recv_sem.at[index],
            device_id={"expert": device}, device_id_type=MESH,
        )
        copies[key].start()

    def got(*keys):
        for key in keys:
            if key not in landed:
                landed.add(key)
                copies[key].wait_recv()

    local_count = [0]

    def local(src, dst):
        made = pltpu.make_async_copy(src, dst, local_sem.at[local_count[0]])
        local_count[0] += 1
        made.start()
        return made

    barrier = pltpu.get_barrier_semaphore()
    for device in (x_plus, x_minus, y_plus, y_minus):
        pl.semaphore_signal(barrier, inc=1, device_id={"expert": device}, device_id_type=MESH)
    own_in = [local(tokens.at[pl.ds(s * half, half)], own.at[s]) for s in range(2)]
    small_in = [
        local(routing, route_v), local(priority, prio_v), local(hot_list, hot_s), local(router, w_router)
    ]
    pl.semaphore_wait(barrier, 4)

    def settle(left, keep):
        while len(left) > keep:
            left.pop(0).wait_send()

    def own_first(s):
        block = tokens.at[pl.ds(s * half, half)]
        remote(("O+", s), block, grid_tok.at[3, s, 0], first[s][0])
        remote(("O-", s), block, grid_tok.at[1, s, 0], first[s][1])

    def spread(d, s):
        if d == 0:
            block = tokens.at[pl.ds(s * half, half)]
        else:
            got(*{3: [("O+", s)], 1: [("O-", s)], 2: [("f+", s), ("f-", s)]}[d])
            block = grid_tok.at[d, s, 0]
        remote(("S+", d, s), block, grid_tok.at[d, s, 3], second[s][0])
        remote(("S-", d, s), block, grid_tok.at[d, s, 1], second[s][1])

    def pass_first(plus, s):
        if plus:
            got(("O+", s))
            remote(("f+", s), grid_tok.at[3, s, 0, LO], grid_tok.at[2, s, 0, LO], first[s][0])
        else:
            got(("O-", s))
            remote(("f-", s), grid_tok.at[1, s, 0, HI], grid_tok.at[2, s, 0, HI], first[s][1])

    def pass_second(plus, d, s):
        if plus:
            got(("S+", d, s))
            remote(("g+", d, s), grid_tok.at[d, s, 3, LO], grid_tok.at[d, s, 2, LO], second[s][0])
        else:
            got(("S-", d, s))
            remote(("g-", d, s), grid_tok.at[d, s, 1, HI], grid_tok.at[d, s, 2, HI], second[s][1])

    def share_x():
        make_shares()
        pl.semaphore_wait(far_sem.at[0], 1)
        remote("X+", shares.at[0, 0], shares.at[3, 0], x_plus)
        remote("X-", shares.at[0, 0], shares.at[1, 0], x_minus)
        remote("X2", shares.at[0, 0], shares.at[2, 0], x_far)

    def share_y():
        got("X+", "X-", "X2")
        pl.semaphore_wait(far_sem.at[1], 1)
        remote("Y+", shares.at[:, 0], shares.at[:, 3], y_plus)
        remote("Y-", shares.at[:, 0], shares.at[:, 1], y_minus)
        remote("Y2", shares.at[:, 0], shares.at[:, 2], y_far)

    my_row, my_half = me % 8, me // 8
    rows = SIDE * half
    loaded = []

    def expert(d, s):
        if not loaded:
            got("X+", "X-", "X2", "Y+", "Y-", "Y2")
            for made in heavy_in:
                made.wait()
            loaded.append(1)
        got(("S+", d, s), ("S-", d, s), ("g+", d, s), ("g-", d, s))
        got(*{0: [], 3: [("O+", s)], 1: [("O-", s)], 2: [("f+", s), ("f-", s)]}[d])
        share_row = lax.broadcasted_iota(jnp.int32, (8, 128), 0) == my_row
        token_lane = lax.broadcasted_iota(jnp.int32, (half, 128), 1)
        token_row = lax.broadcasted_iota(jnp.int32, (half, 128), 0)
        pick = token_lane == token_row + (my_half * 64 + s * half)
        for e in range(SIDE):
            held = shares[d, e] if s == 0 else shares[e, d]
            row = jnp.sum(jnp.where(share_row, held, 0.0), axis=0, keepdims=True)
            row = jnp.broadcast_to(row, (half, 128))
            columns[pl.ds(e * half, half)] = jnp.broadcast_to(
                jnp.sum(jnp.where(pick, row, 0.0), axis=1, keepdims=True), (half, 128)
            )
        for n in range(n_ff // 256):
            at = pl.ds(n * 256, 256)
            block = grid_tok[d, s].reshape(rows, width)
            g = jnp.dot(block, w_gate[:, at], preferred_element_type=jnp.float32)
            u = jnp.dot(block, w_up[:, at], preferred_element_type=jnp.float32)
            hidden[:, at] = (g / (1.0 + jnp.exp(-g)) * u).astype(jnp.bfloat16)
        for n in range(width // 256):
            at = pl.ds(n * 256, 256)
            o = jnp.dot(hidden[...], w_down[:, at], preferred_element_type=jnp.float32)
            scale = jnp.concatenate([columns[...], columns[...]], axis=1)
            part[d, s, :, :, at] = (o * scale).astype(jnp.bfloat16).reshape(SIDE, half, 256)

    def total(*values):
        result = values[0].astype(jnp.float32)
        for value in values[1:]:
            result = result + value.astype(jnp.float32)
        return result

    def far_halves(d, s):
        remote(("a+", d, s), part.at[d, s, 2, LO], relay.at[d, s, 0], second[s][0])
        remote(("a-", d, s), part.at[d, s, 2, HI], relay.at[d, s, 1], second[s][1])

    def near_halves(d, s):
        remote(("b+", d, s), part.at[d, s, 1, HI], final.at[d, s, 0, HI], second[s][0])
        remote(("b-", d, s), part.at[d, s, 3, LO], final.at[d, s, 1, LO], second[s][1])

    def add_second(plus, d, s):
        if plus:
            got(("a+", d, s))
            part[d, s, 1, LO] = total(part[d, s, 1, LO], relay[d, s, 0]).astype(jnp.bfloat16)
            remote(("r+", d, s), part.at[d, s, 1, LO], final.at[d, s, 0, LO], second[s][0])
        else:
            got(("a-", d, s))
            part[d, s, 3, HI] = total(part[d, s, 3, HI], relay[d, s, 1]).astype(jnp.bfloat16)
            remote(("r-", d, s), part.at[d, s, 3, HI], final.at[d, s, 1, HI], second[s][1])

    def fold(d, s):
        got(("b+", d, s), ("b-", d, s), ("r+", d, s), ("r-", d, s))
        summed[d, s] = total(part[d, s, 0], final[d, s, 0], final[d, s, 1]).astype(jnp.bfloat16)

    def far_first(s):
        remote(("A+", s), summed.at[2, s, LO], relay2.at[s, 0], first[s][0])
        remote(("A-", s), summed.at[2, s, HI], relay2.at[s, 1], first[s][1])

    def near_first(plus, s):
        if plus:
            remote(("B+", s), summed.at[1, s, HI], final2.at[s, 0, HI], first[s][0])
        else:
            remote(("B-", s), summed.at[3, s, LO], final2.at[s, 1, LO], first[s][1])

    def add_first(plus, s):
        if plus:
            got(("A+", s))
            summed[1, s, LO] = total(summed[1, s, LO], relay2[s, 0]).astype(jnp.bfloat16)
            remote(("R+", s), summed.at[1, s, LO], final2.at[s, 0, LO], first[s][0])
        else:
            got(("A-", s))
            summed[3, s, HI] = total(summed[3, s, HI], relay2[s, 1]).astype(jnp.bfloat16)
            remote(("R-", s), summed.at[3, s, HI], final2.at[s, 1, HI], first[s][1])

    def fold_own(s):
        got(("b+", 0, s), ("b-", 0, s), ("r+", 0, s), ("r-", 0, s))
        mine[s] = total(part[0, s, 0], final[0, s, 0], final[0, s, 1])

    def finish(s):
        got(("B+", s), ("B-", s), ("R+", s), ("R-", s))
        out[pl.ds(s * half, half)] = total(mine[s], final2[s, 0], final2[s, 1]).astype(jnp.bfloat16)

    def make_shares():
        for made in own_in + small_in:
            made.wait()
        toks = 2 * half
        contract = (((1,), (1,)), ((), ()))
        logits = jnp.concatenate(
            [
                lax.dot_general(w_router[...], own[s], contract, preferred_element_type=jnp.float32)
                for s in range(2)
            ]
            + [jnp.zeros((n_exp, 128 - toks), jnp.float32)],
            axis=1,
        )
        sigmas = jax.nn.sigmoid(logits)
        experts = lax.broadcasted_iota(jnp.int32, (n_exp, 128), 0)
        slots = prio_v.shape[1]
        slot_at = lax.broadcasted_iota(jnp.int32, (slots, 128), 0)
        slot_of = lax.broadcasted_iota(jnp.int32, (slots, 128), 1) * SIDE
        order = jnp.broadcast_to(prio_v[...].astype(jnp.float32), (8, slots)).astype(jnp.bfloat16)
        prior = jnp.full((n_exp, 128), FAR, jnp.float32)
        picked = jnp.zeros((n_exp, 128), jnp.float32)
        for k in range(route_v.shape[0]):
            chosen = jnp.concatenate(
                [route_v[k : k + 1, :], jnp.full((1, 128 - toks), -1, jnp.int32)], axis=1
            )
            hit = chosen == experts
            select = jnp.where(slot_at == slot_of + k, 1.0, 0.0).astype(jnp.bfloat16)
            place = jnp.dot(order, select, preferred_element_type=jnp.float32)[:1]
            prior = jnp.where(hit, place, prior)
            picked = jnp.where(hit, sigmas, picked)
        weights = picked / jnp.sum(picked, axis=0, keepdims=True)
        prior_t = jnp.transpose(
            jnp.concatenate([prior, jnp.full((128 - n_exp, 128), FAR, jnp.float32)], axis=0)
        )[:toks]
        rank_rows = []
        for e in range(n_exp):
            before = prior_t[:, e : e + 1] < prior[e : e + 1, :]
            rank_rows.append(jnp.sum(jnp.where(before, 1.0, 0.0), axis=0, keepdims=True))
        ranks = jnp.concatenate(rank_rows, axis=0)
        hot = (experts == hot_s[0]) | (experts == hot_s[1])
        token_at = lax.broadcasted_iota(jnp.int32, (n_exp, 128), 1)
        keep = (hot | (ranks < capacity)) & (token_at < toks)
        kept = jnp.where(keep, weights, 0.0)
        shares[0, 0] = kept[:8] + pltpu.roll(kept[8:], 64, axis=1)

    run = {
        "O": own_first, "S": spread, "f": pass_first, "g": pass_second, "X": share_x, "Y": share_y,
        "E": expert, "a": far_halves, "b": near_halves, "r": add_second, "F": fold, "A": far_first,
        "B": near_first, "R": add_first, "P": fold_own, "Z": finish,
    }
    heavy_in, left = [], []
    for at, step in enumerate(ORDER):
        if at == 4:
            pl.semaphore_signal(
                far_sem.at[0], inc=1, device_id={"expert": x_plus}, device_id_type=MESH
            )
            pl.semaphore_signal(
                far_sem.at[1], inc=1, device_id={"expert": y_plus}, device_id_type=MESH
            )
            heavy_in += [
                local(tokens.at[pl.ds(s * half, half)], grid_tok.at[0, s, 0]) for s in range(2)
            ]
            heavy_in += [
                local(gate.at[0], w_gate), local(up.at[0], w_up), local(down.at[0], w_down)
            ]
        before = len(copies)
        if step[0] == "P":
            settle(left, 12)
        run[step[0]](*step[1:])
        left += list(copies.values())[before:]
        settle(left, 40)
    assert len(landed) == len(copies)
    settle(left, 0)


def shards(tokens, router_weight, gate_weight, up_weight, down_weight, routing, priority, hot_list):
    toks, width = tokens.shape
    half = toks // 2
    n_ff = gate_weight.shape[2]
    bf16, f32 = jnp.bfloat16, jnp.float32
    hbm = pl.BlockSpec(memory_space=pltpu.HBM)
    return pl.pallas_call(
        kernel,
        out_shape=jax.ShapeDtypeStruct((toks, width), bf16),
        in_specs=[hbm] * 8,
        out_specs=pl.BlockSpec(memory_space=pltpu.VMEM),
        scratch_shapes=[
            pltpu.VMEM((SIDE, 2, SIDE, half, width), bf16),
            pltpu.VMEM((SIDE, 2, SIDE, half, width), bf16),
            pltpu.VMEM((SIDE, 2, 2, half // 2, width), bf16),
            pltpu.VMEM((SIDE, 2, 2, half, width), bf16),
            pltpu.VMEM((SIDE, 2, half, width), bf16),
            pltpu.VMEM((2, 2, half // 2, width), bf16),
            pltpu.VMEM((2, 2, half, width), bf16),
            pltpu.VMEM((SIDE, SIDE, 8, 128), f32),
            pltpu.VMEM((SIDE * half, 128), f32),
            pltpu.VMEM((width, n_ff), bf16),
            pltpu.VMEM((width, n_ff), bf16),
            pltpu.VMEM((n_ff, width), bf16),
            pltpu.VMEM(router_weight.shape[::-1], bf16),
            pltpu.VMEM((2, half, width), bf16),
            pltpu.VMEM((2, half, width), f32),
            pltpu.VMEM((SIDE * half, n_ff), bf16),
            pltpu.VMEM(routing.shape[::-1], jnp.int32),
            pltpu.VMEM(priority.shape, jnp.int32),
            pltpu.SMEM(hot_list.shape, jnp.int32),
            pltpu.SemaphoreType.DMA((N_SEMS,)),
            pltpu.SemaphoreType.DMA((N_SEMS,)),
            pltpu.SemaphoreType.DMA((16,)),
            pltpu.SemaphoreType.REGULAR((2,)),
        ],
        compiler_params=pltpu.CompilerParams(
            collective_id=0, has_side_effects=True, vmem_limit_bytes=51683328
        ),
    )(*(pltpu.with_memory_space_constraint(v, pltpu.HBM) for v in (
        tokens, router_weight.T, gate_weight, up_weight, down_weight, routing.T, priority, hot_list
    )))


def solution(mesh):
    return jax.shard_map(
        shards,
        mesh=mesh,
        in_specs=(
            P(("dp", "expert"), None),
            P(),
            P("expert", None, None),
            P("expert", None, None),
            P("expert", None, None),
            P(("dp", "expert"), None),
            P(("dp", "expert"), None),
            P("dp"),
        ),
        out_specs=P(("dp", "expert"), None),
        check_vma=False,
    )
```

```python
import jax
import jax.numpy as jnp
from jax import lax
from jax.experimental import pallas as pl
from jax.experimental.pallas import tpu as pltpu
from jax.sharding import PartitionSpec as P

MESH = pl.DeviceIdType.MESH
SIDE = 4
LO, HI = pl.ds(0, 16), pl.ds(16, 16)
N_SEMS = 128
FAR = 4096.0
ORDER = (
    ("O", 0), ("O", 1), ("S", 0, 1), ("S", 0, 0), ("X",), ("S", 3, 0), ("S", 1, 1), ("f", 1, 1),
    ("f", 1, 0), ("f", 0, 0), ("g", 0, 0, 1), ("f", 0, 1), ("Y",), ("g", 1, 0, 1), ("S", 1, 0),
    ("g", 1, 3, 0), ("g", 0, 3, 0), ("g", 0, 1, 1), ("g", 1, 1, 1), ("S", 2, 1), ("S", 3, 1),
    ("S", 2, 0), ("E", 0, 1), ("D", 0, 1), ("g", 1, 1, 0), ("g", 1, 0, 0), ("g", 0, 1, 0), ("E", 1, 1),
    ("D", 1, 1), ("g", 0, 2, 1), ("g", 1, 2, 1), ("a", 1, 1), ("a", 0, 1), ("g", 0, 0, 0), ("E", 3, 0),
    ("D", 3, 0), ("g", 0, 2, 0), ("g", 1, 2, 0), ("a", 3, 0), ("b", 3, 0), ("g", 1, 3, 1), ("b", 1, 1),
    ("g", 0, 3, 1), ("E", 1, 0), ("D", 1, 0), ("b", 1, 0), ("a", 1, 0), ("E", 2, 1), ("D", 2, 1),
    ("a", 2, 1), ("b", 2, 1), ("E", 2, 0), ("D", 2, 0), ("a", 2, 0), ("r", 0, 0, 1), ("r", 1, 1, 1),
    ("b", 2, 0), ("E", 3, 1), ("D", 3, 1), ("a", 3, 1), ("r", 1, 3, 0), ("r", 1, 2, 1), ("r", 0, 3, 0),
    ("r", 1, 0, 1), ("r", 0, 2, 1), ("r", 0, 1, 1), ("r", 0, 2, 0), ("r", 1, 2, 0), ("r", 1, 1, 0),
    ("b", 3, 1), ("r", 0, 1, 0), ("E", 0, 0), ("D", 0, 0), ("a", 0, 0), ("r", 1, 3, 1), ("r", 0, 3, 1),
    ("F", 2, 1), ("A", 1), ("F", 2, 0), ("A", 0), ("b", 0, 0), ("F", 1, 1), ("F", 3, 0), ("B", 0, 0),
    ("b", 0, 1), ("B", 1, 1), ("r", 0, 0, 0), ("F", 1, 0), ("B", 1, 0), ("r", 1, 0, 0), ("F", 3, 1),
    ("R", 0, 1), ("R", 1, 1), ("R", 0, 0), ("R", 1, 0), ("B", 0, 1), ("P", 1), ("P", 0), ("Z", 0),
    ("Z", 1),
)


def kernel(
    tokens, router, gate, up, down, routing, priority, hot_list, out,
    grid_tok, part, relay, final, summed, relay2, final2, shares, columns,
    w_gate, w_up, w_down, w_router, own, mine, hidden, route_v, prio_v, hot_s,
    send_sem, recv_sem, local_sem, far_sem,
):
    me = lax.axis_index("expert")
    my_y, my_x = me // SIDE, me % SIDE
    x_plus = my_y * SIDE + (my_x + 1) % SIDE
    x_minus = my_y * SIDE + (my_x + SIDE - 1) % SIDE
    y_plus = ((my_y + 1) % SIDE) * SIDE + my_x
    y_minus = ((my_y + SIDE - 1) % SIDE) * SIDE + my_x
    x_far = my_y * SIDE + (my_x + 2) % SIDE
    y_far = ((my_y + 2) % SIDE) * SIDE + my_x
    first = ((x_plus, x_minus), (y_plus, y_minus))
    second = ((y_plus, y_minus), (x_plus, x_minus))
    half = own.shape[1]
    n_ff = w_gate.shape[1]
    width = w_gate.shape[0]
    n_exp = SIDE * SIDE
    capacity = min(2 * half, 3 * prio_v.shape[1] // (2 * n_exp))

    copies, landed = {}, set()

    def remote(key, src, dst, device):
        index = len(copies)
        copies[key] = pltpu.make_async_remote_copy(
            src_ref=src, dst_ref=dst, send_sem=send_sem.at[index], recv_sem=recv_sem.at[index],
            device_id={"expert": device}, device_id_type=MESH,
        )
        copies[key].start()

    def got(*keys):
        for key in keys:
            if key not in landed:
                landed.add(key)
                copies[key].wait_recv()

    local_count = [0]

    def local(src, dst):
        made = pltpu.make_async_copy(src, dst, local_sem.at[local_count[0]])
        local_count[0] += 1
        made.start()
        return made

    barrier = pltpu.get_barrier_semaphore()
    for device in (x_plus, x_minus, y_plus, y_minus):
        pl.semaphore_signal(barrier, inc=1, device_id={"expert": device}, device_id_type=MESH)
    own_in = [local(tokens.at[pl.ds(s * half, half)], own.at[s]) for s in range(2)]
    small_in = [
        local(routing, route_v), local(priority, prio_v), local(hot_list, hot_s), local(router, w_router)
    ]
    pl.semaphore_wait(barrier, 4)

    def settle(left, keep):
        while len(left) > keep:
            left.pop(0).wait_send()

    def own_first(s):
        block = tokens.at[pl.ds(s * half, half)]
        remote(("O+", s), block, grid_tok.at[3, s, 0], first[s][0])
        remote(("O-", s), block, grid_tok.at[1, s, 0], first[s][1])

    def spread(d, s):
        if d == 0:
            block = tokens.at[pl.ds(s * half, half)]
        else:
            got(*{3: [("O+", s)], 1: [("O-", s)], 2: [("f+", s), ("f-", s)]}[d])
            block = grid_tok.at[d, s, 0]
        remote(("S+", d, s), block, grid_tok.at[d, s, 3], second[s][0])
        remote(("S-", d, s), block, grid_tok.at[d, s, 1], second[s][1])

    def pass_first(plus, s):
        if plus:
            got(("O+", s))
            remote(("f+", s), grid_tok.at[3, s, 0, LO], grid_tok.at[2, s, 0, LO], first[s][0])
        else:
            got(("O-", s))
            remote(("f-", s), grid_tok.at[1, s, 0, HI], grid_tok.at[2, s, 0, HI], first[s][1])

    def pass_second(plus, d, s):
        if plus:
            got(("S+", d, s))
            remote(("g+", d, s), grid_tok.at[d, s, 3, LO], grid_tok.at[d, s, 2, LO], second[s][0])
        else:
            got(("S-", d, s))
            remote(("g-", d, s), grid_tok.at[d, s, 1, HI], grid_tok.at[d, s, 2, HI], second[s][1])

    def share_x():
        make_shares()
        pl.semaphore_wait(far_sem.at[0], 1)
        remote("X+", shares.at[0, 0], shares.at[3, 0], x_plus)
        remote("X-", shares.at[0, 0], shares.at[1, 0], x_minus)
        remote("X2", shares.at[0, 0], shares.at[2, 0], x_far)

    def share_y():
        got("X+", "X-", "X2")
        pl.semaphore_wait(far_sem.at[1], 1)
        remote("Y+", shares.at[:, 0], shares.at[:, 3], y_plus)
        remote("Y-", shares.at[:, 0], shares.at[:, 1], y_minus)
        remote("Y2", shares.at[:, 0], shares.at[:, 2], y_far)

    my_row, my_half = me % 8, me // 8
    rows = SIDE * half
    loaded = []

    def hidden_block(d, s):
        if not loaded:
            for made in heavy_in:
                made.wait()
            loaded.append(1)
        got(("S+", d, s), ("S-", d, s), ("g+", d, s), ("g-", d, s))
        got(*{0: [], 3: [("O+", s)], 1: [("O-", s)], 2: [("f+", s), ("f-", s)]}[d])
        block = grid_tok[d, s].reshape(rows, width)
        for n in range(n_ff // 256):
            at = pl.ds(n * 256, 256)
            g = jnp.dot(block, w_gate[:, at], preferred_element_type=jnp.float32)
            u = jnp.dot(block, w_up[:, at], preferred_element_type=jnp.float32)
            hidden[d, s, :, at] = (g / (1.0 + jnp.exp(-g)) * u).astype(jnp.bfloat16)

    def answer_block(d, s):
        got("X+", "X-", "X2", "Y+", "Y-", "Y2")
        share_row = lax.broadcasted_iota(jnp.int32, (8, 128), 0) == my_row
        token_lane = lax.broadcasted_iota(jnp.int32, (half, 128), 1)
        token_row = lax.broadcasted_iota(jnp.int32, (half, 128), 0)
        pick = token_lane == token_row + (my_half * 64 + s * half)
        for e in range(SIDE):
            held = shares[d, e] if s == 0 else shares[e, d]
            row = jnp.sum(jnp.where(share_row, held, 0.0), axis=0, keepdims=True)
            row = jnp.broadcast_to(row, (half, 128))
            columns[pl.ds(e * half, half)] = jnp.broadcast_to(
                jnp.sum(jnp.where(pick, row, 0.0), axis=1, keepdims=True), (half, 128)
            )
        for n in range(width // 256):
            at = pl.ds(n * 256, 256)
            o = jnp.dot(hidden[d, s], w_down[:, at], preferred_element_type=jnp.float32)
            scale = jnp.concatenate([columns[...], columns[...]], axis=1)
            part[d, s, :, :, at] = (o * scale).astype(jnp.bfloat16).reshape(SIDE, half, 256)

    def total(*values):
        result = values[0].astype(jnp.float32)
        for value in values[1:]:
            result = result + value.astype(jnp.float32)
        return result

    def far_halves(d, s):
        remote(("a+", d, s), part.at[d, s, 2, LO], relay.at[d, s, 0], second[s][0])
        remote(("a-", d, s), part.at[d, s, 2, HI], relay.at[d, s, 1], second[s][1])

    def near_halves(d, s):
        remote(("b+", d, s), part.at[d, s, 1, HI], final.at[d, s, 0, HI], second[s][0])
        remote(("b-", d, s), part.at[d, s, 3, LO], final.at[d, s, 1, LO], second[s][1])

    def add_second(plus, d, s):
        if plus:
            got(("a+", d, s))
            part[d, s, 1, LO] = total(part[d, s, 1, LO], relay[d, s, 0]).astype(jnp.bfloat16)
            remote(("r+", d, s), part.at[d, s, 1, LO], final.at[d, s, 0, LO], second[s][0])
        else:
            got(("a-", d, s))
            part[d, s, 3, HI] = total(part[d, s, 3, HI], relay[d, s, 1]).astype(jnp.bfloat16)
            remote(("r-", d, s), part.at[d, s, 3, HI], final.at[d, s, 1, HI], second[s][1])

    def fold(d, s):
        got(("b+", d, s), ("b-", d, s), ("r+", d, s), ("r-", d, s))
        summed[d, s] = total(part[d, s, 0], final[d, s, 0], final[d, s, 1]).astype(jnp.bfloat16)

    def far_first(s):
        remote(("A+", s), summed.at[2, s, LO], relay2.at[s, 0], first[s][0])
        remote(("A-", s), summed.at[2, s, HI], relay2.at[s, 1], first[s][1])

    def near_first(plus, s):
        if plus:
            remote(("B+", s), summed.at[1, s, HI], final2.at[s, 0, HI], first[s][0])
        else:
            remote(("B-", s), summed.at[3, s, LO], final2.at[s, 1, LO], first[s][1])

    def add_first(plus, s):
        if plus:
            got(("A+", s))
            summed[1, s, LO] = total(summed[1, s, LO], relay2[s, 0]).astype(jnp.bfloat16)
            remote(("R+", s), summed.at[1, s, LO], final2.at[s, 0, LO], first[s][0])
        else:
            got(("A-", s))
            summed[3, s, HI] = total(summed[3, s, HI], relay2[s, 1]).astype(jnp.bfloat16)
            remote(("R-", s), summed.at[3, s, HI], final2.at[s, 1, HI], first[s][1])

    def fold_own(s):
        got(("b+", 0, s), ("b-", 0, s), ("r+", 0, s), ("r-", 0, s))
        mine[s] = total(part[0, s, 0], final[0, s, 0], final[0, s, 1])

    def finish(s):
        got(("B+", s), ("B-", s), ("R+", s), ("R-", s))
        out[pl.ds(s * half, half)] = total(mine[s], final2[s, 0], final2[s, 1]).astype(jnp.bfloat16)

    def make_shares():
        for made in own_in + small_in:
            made.wait()
        toks = 2 * half
        contract = (((1,), (1,)), ((), ()))
        logits = jnp.concatenate(
            [
                lax.dot_general(w_router[...], own[s], contract, preferred_element_type=jnp.float32)
                for s in range(2)
            ]
            + [jnp.zeros((n_exp, 128 - toks), jnp.float32)],
            axis=1,
        )
        sigmas = jax.nn.sigmoid(logits)
        experts = lax.broadcasted_iota(jnp.int32, (n_exp, 128), 0)
        slots = prio_v.shape[1]
        slot_at = lax.broadcasted_iota(jnp.int32, (slots, 128), 0)
        slot_of = lax.broadcasted_iota(jnp.int32, (slots, 128), 1) * SIDE
        order = jnp.broadcast_to(prio_v[...].astype(jnp.float32), (8, slots)).astype(jnp.bfloat16)
        prior = jnp.full((n_exp, 128), FAR, jnp.float32)
        picked = jnp.zeros((n_exp, 128), jnp.float32)
        for k in range(route_v.shape[0]):
            chosen = jnp.concatenate(
                [route_v[k : k + 1, :], jnp.full((1, 128 - toks), -1, jnp.int32)], axis=1
            )
            hit = chosen == experts
            select = jnp.where(slot_at == slot_of + k, 1.0, 0.0).astype(jnp.bfloat16)
            place = jnp.dot(order, select, preferred_element_type=jnp.float32)[:1]
            prior = jnp.where(hit, place, prior)
            picked = jnp.where(hit, sigmas, picked)
        weights = picked / jnp.sum(picked, axis=0, keepdims=True)
        prior_t = jnp.transpose(
            jnp.concatenate([prior, jnp.full((128 - n_exp, 128), FAR, jnp.float32)], axis=0)
        )[:toks]
        rank_rows = []
        for e in range(n_exp):
            before = prior_t[:, e : e + 1] < prior[e : e + 1, :]
            rank_rows.append(jnp.sum(jnp.where(before, 1.0, 0.0), axis=0, keepdims=True))
        ranks = jnp.concatenate(rank_rows, axis=0)
        hot = (experts == hot_s[0]) | (experts == hot_s[1])
        token_at = lax.broadcasted_iota(jnp.int32, (n_exp, 128), 1)
        keep = (hot | (ranks < capacity)) & (token_at < toks)
        kept = jnp.where(keep, weights, 0.0)
        shares[0, 0] = kept[:8] + pltpu.roll(kept[8:], 64, axis=1)

    run = {
        "O": own_first, "S": spread, "f": pass_first, "g": pass_second, "X": share_x, "Y": share_y,
        "E": hidden_block, "D": answer_block, "a": far_halves, "b": near_halves, "r": add_second, "F": fold, "A": far_first,
        "B": near_first, "R": add_first, "P": fold_own, "Z": finish,
    }
    heavy_in, left = [], []
    for at, step in enumerate(ORDER):
        if at == 4:
            pl.semaphore_signal(
                far_sem.at[0], inc=1, device_id={"expert": x_plus}, device_id_type=MESH
            )
            pl.semaphore_signal(
                far_sem.at[1], inc=1, device_id={"expert": y_plus}, device_id_type=MESH
            )
            heavy_in += [
                local(tokens.at[pl.ds(s * half, half)], grid_tok.at[0, s, 0]) for s in range(2)
            ]
            heavy_in += [
                local(gate.at[0], w_gate), local(up.at[0], w_up), local(down.at[0], w_down)
            ]
        before = len(copies)
        if step[0] == "P":
            settle(left, 12)
        run[step[0]](*step[1:])
        left += list(copies.values())[before:]
        settle(left, 40)
    assert len(landed) == len(copies)
    settle(left, 0)


def shards(tokens, router_weight, gate_weight, up_weight, down_weight, routing, priority, hot_list):
    toks, width = tokens.shape
    half = toks // 2
    n_ff = gate_weight.shape[2]
    bf16, f32 = jnp.bfloat16, jnp.float32
    hbm = pl.BlockSpec(memory_space=pltpu.HBM)
    return pl.pallas_call(
        kernel,
        out_shape=jax.ShapeDtypeStruct((toks, width), bf16),
        in_specs=[hbm] * 8,
        out_specs=pl.BlockSpec(memory_space=pltpu.VMEM),
        scratch_shapes=[
            pltpu.VMEM((SIDE, 2, SIDE, half, width), bf16),
            pltpu.VMEM((SIDE, 2, SIDE, half, width), bf16),
            pltpu.VMEM((SIDE, 2, 2, half // 2, width), bf16),
            pltpu.VMEM((SIDE, 2, 2, half, width), bf16),
            pltpu.VMEM((SIDE, 2, half, width), bf16),
            pltpu.VMEM((2, 2, half // 2, width), bf16),
            pltpu.VMEM((2, 2, half, width), bf16),
            pltpu.VMEM((SIDE, SIDE, 8, 128), f32),
            pltpu.VMEM((SIDE * half, 128), f32),
            pltpu.VMEM((width, n_ff), bf16),
            pltpu.VMEM((width, n_ff), bf16),
            pltpu.VMEM((n_ff, width), bf16),
            pltpu.VMEM(router_weight.shape[::-1], bf16),
            pltpu.VMEM((2, half, width), bf16),
            pltpu.VMEM((2, half, width), f32),
            pltpu.VMEM((SIDE, 2, SIDE * half, n_ff), bf16),
            pltpu.VMEM(routing.shape[::-1], jnp.int32),
            pltpu.VMEM(priority.shape, jnp.int32),
            pltpu.SMEM(hot_list.shape, jnp.int32),
            pltpu.SemaphoreType.DMA((N_SEMS,)),
            pltpu.SemaphoreType.DMA((N_SEMS,)),
            pltpu.SemaphoreType.DMA((16,)),
            pltpu.SemaphoreType.REGULAR((2,)),
        ],
        compiler_params=pltpu.CompilerParams(
            collective_id=0, has_side_effects=True, vmem_limit_bytes=51683328
        ),
    )(*(pltpu.with_memory_space_constraint(v, pltpu.HBM) for v in (
        tokens, router_weight.T, gate_weight, up_weight, down_weight, routing.T, priority, hot_list
    )))


def solution(mesh):
    return jax.shard_map(
        shards,
        mesh=mesh,
        in_specs=(
            P(("dp", "expert"), None),
            P(),
            P("expert", None, None),
            P("expert", None, None),
            P("expert", None, None),
            P(("dp", "expert"), None),
            P(("dp", "expert"), None),
            P("dp"),
        ),
        out_specs=P(("dp", "expert"), None),
        check_vma=False,
    )
```
